256 devices in a mesh: agg: 64 (over x, z, core), col: 4 (over y).
Axes of the slice: x: 4, y: 4, z: 8, core: 2. Of those that a mesh axis runs over, the one named last changes fastest.
Arguments:
- fine_tiles: bfloat16 [1024, 4, 192, 192], P('agg', 'col')
- fine_cols: int32 [1024, 4], P('agg', 'col'), may hold values from 0 to 1023, as said below
- agg_of: int32 [1024], P('agg'), may hold values from 0 to 255, as said below
- prolong: bfloat16 [1024, 192, 192], P('agg'), may hold values from -0.21875 to 0.21875
- coarse_cols: int32 [256, 4], P('agg'), may hold values from 0 to 255, as said below
Outputs:
- coarse_tiles: float32 [256, 4, 192, 192], P('agg', 'col')
- factor_tiles: float32 [256, 4, 192, 192], P('agg', 'col')
The draws below stay inside these ranges and needn't reach their ends.
Inputs may be any that keep to these rules, and one draw needn't show every extreme that they name: Fine block row i belongs to an aggregate of its own index of agg: i // 16 * 4 <= agg_of[i] < i // 16 * 4 + 4; every aggregate has at least one fine row. `coarse_cols`: slot 0 of aggregate row c is c itself; the other slots are distinct aggregates c + o with 1 <= |o| <= 4. `fine_cols`: slot 0 of fine row i is i; for slots 1 and above the aggregate of the named fine row is one of the slots 1 and above of row agg_of[i] of coarse_cols.
All inputs are finite; a program needn't handle non-finite values.
Results may differ from the reference program's by a relative error of at most 0.0055.
Values may be sent and summed in bfloat16 or wider, within the bound.
No kernel may reach another device: no remote copies, remote signals or barrier semaphores. Data moves between devices by JAX's collectives and lax.ppermute only.
A program may use at most 128 MiB of HBM per device.

```python
import math
import jax
import jax.numpy as jnp
from jax import lax

B = 192
NA = 4
NC = 4
COARSE_DEV = 4
FR_DEV = 16
SWEEPS = 2
FINE = 1024
COARSE = 256
N_AGG = 64


def pattern_table(key):
    reach = COARSE_DEV
    row_ids = jnp.arange(COARSE, dtype=jnp.int32)
    offsets = jnp.concatenate([jnp.arange(-reach, 0, dtype=jnp.int32), jnp.arange(1, reach + 1, dtype=jnp.int32)])
    places = row_ids[:, None] + offsets[None, :]
    inside = (places >= 0) & (places < COARSE)
    positions = jnp.arange(2 * reach, dtype=jnp.int32)
    scores = jax.random.randint(jax.random.fold_in(key, 11), (COARSE, 2 * reach), 0, 1 << 20) * (2 * reach) + positions[None, :]
    scores = jnp.where(inside, scores, -1 - positions[None, :])
    unused, picked = lax.top_k(scores, NC - 1)
    chosen = jnp.take_along_axis(places, picked, axis=1)
    return jnp.concatenate([row_ids[:, None], chosen], axis=1).astype(jnp.int32)


def grouping(key):
    groups = COARSE // COARSE_DEV
    positions = jnp.arange(FR_DEV, dtype=jnp.int32)
    scores = jax.random.randint(jax.random.fold_in(key, 23), (groups, FR_DEV), 0, 1 << 20) * FR_DEV + positions[None, :]
    permuted = jnp.argsort(scores, axis=1, stable=True).astype(jnp.int32)
    extra = jax.random.randint(jax.random.fold_in(key, 29), (groups, FR_DEV), 0, COARSE_DEV)
    labels = jnp.where(positions[None, :] < COARSE_DEV, positions[None, :], extra)
    ranking = jnp.argsort(permuted, axis=1, stable=True).astype(jnp.int32)
    local_label = jnp.take_along_axis(labels, ranking, axis=1)
    owners = jnp.arange(groups, dtype=jnp.int32)[:, None] * COARSE_DEV
    return ((local_label + owners).reshape(-1).astype(jnp.int32), permuted)


def draw_coarse_cols(key, part):
    return pattern_table(key)


def draw_agg_of(key, part):
    assigned, permuted = grouping(key)
    return assigned


def draw_fine_cols(key, part):
    pattern = pattern_table(key)
    assigned, permuted = grouping(key)
    row_ids = jnp.arange(FINE, dtype=jnp.int32)
    picked = jax.random.randint(jax.random.fold_in(key, 31), (FINE, NA - 1), 1, NC)
    target = pattern[assigned[:, None], picked]
    host_dev = target // COARSE_DEV
    member = target % COARSE_DEV
    attempts = jax.random.randint(jax.random.fold_in(key, 37), (FINE, NA - 1, 8), 0, FR_DEV)
    guesses = host_dev[..., None] * FR_DEV + attempts
    matches = assigned[guesses] == target[..., None]
    first_hit = jnp.argmax(matches.astype(jnp.int32), axis=-1)
    found = jnp.take_along_axis(guesses, first_hit[..., None], axis=-1)[..., 0]
    fallback = host_dev * FR_DEV + permuted[host_dev, member]
    chosen = jnp.where(jnp.any(matches, axis=-1), found, fallback)
    return jnp.concatenate([row_ids[:, None], chosen], axis=1).astype(jnp.int32)


def draw_fine_tiles(key, part):
    spread = 4.0 / math.sqrt(B)
    tile_shape = (FINE, NA, B, B)
    noise = jax.random.normal(jax.random.fold_in(key, 41), tile_shape, jnp.float32) * spread
    lifting = jnp.exp(jax.random.uniform(jax.random.fold_in(key, 43), (FINE, B), jnp.float32, math.log(0.6), math.log(4.0)))
    identity = jnp.eye(B, dtype=jnp.float32)
    noise = noise.at[:, 0].add(lifting[:, :, None] * identity[None])
    return noise.astype(jnp.bfloat16)


def block_levels(stream_key, shape, pieces, low, largest):
    level, own = 1.0, jax.random.fold_in(stream_key, 6)
    for dim, parts in pieces:
        heights = jnp.exp(jax.random.uniform(jax.random.fold_in(own, dim), (parts,), jnp.float32, low / len(pieces), largest / len(pieces)))
        level = level * jnp.repeat(heights, shape[dim] // parts).reshape([-1 if axis == dim else 1 for axis in range(len(shape))])
    return level


def bell_draw(rng, dims, scale, limit, split=(), kind=jnp.bfloat16):
    drawn = jax.random.normal(rng, dims, jnp.float32) * scale
    if len(split) > 0:
        drawn = block_levels(rng, dims, split, -0.22, 0.18) * drawn
    return jnp.clip(drawn, min=-limit, max=limit).astype(kind)


def setup_inputs(seed: int = 0) -> dict:
    key_of = jax.random.split(jax.random.key(seed), 6)
    fine_tiles = draw_fine_tiles(jax.random.fold_in(key_of[5], 71), 0)
    fine_cols = draw_fine_cols(jax.random.fold_in(key_of[5], 71), 0)
    agg_of = draw_agg_of(jax.random.fold_in(key_of[5], 71), 0)
    prolong = bell_draw(key_of[3], (FINE, B, B), (B * FR_DEV // COARSE_DEV) ** -0.5, 0.21875, ((0, 64),))
    coarse_cols = draw_coarse_cols(jax.random.fold_in(key_of[5], 71), 0)
    return {"fine_tiles": fine_tiles, "fine_cols": fine_cols, "agg_of": agg_of, "prolong": prolong, "coarse_cols": coarse_cols}


HIGHEST = lax.Precision.HIGHEST


def relax_rows(target_coarse, target_old, target_cols, row_full, row_cols, ext_full, ext_cols, row_base, ext_base):
    row_count = row_cols.shape[0]
    ext_count = ext_full.shape[0]
    width = row_full.shape[-1]
    row_ids = row_base + jnp.arange(row_count, dtype=jnp.int32)
    lowest = jnp.minimum(row_ids[:, None], target_cols)
    prior_index = jnp.clip(row_cols - ext_base, 0, ext_count - 1).astype(jnp.int32)
    further = ext_full[prior_index]
    further_cols = ext_cols[prior_index]
    matched = (further_cols[:, None, :, :] == target_cols[:, :, None, None]) & (row_cols[:, None, :, None] < lowest[:, :, None, None])
    chosen = jnp.einsum('rqmn,rmnab->rqmab', matched.astype(jnp.float32), further, precision=HIGHEST)
    through = jnp.einsum('rmab,rqmbc->rqac', row_full, chosen, precision=HIGHEST)
    own_diag = row_full[:, 0]
    diag_index = jnp.clip(target_cols - ext_base, 0, ext_count - 1).astype(jnp.int32)
    their_diag = ext_full[diag_index, 0]
    upper_mask = jnp.arange(width)[None, :] > jnp.arange(width)[:, None]
    lower_mask = upper_mask.T
    upper_tile = row_ids[:, None] < target_cols
    lower_tile = row_ids[:, None] > target_cols
    on_diagonal = row_ids[:, None] == target_cols
    right_factor = jnp.where(upper_tile[:, :, None, None], target_old, jnp.where(upper_mask, own_diag, 0.0)[:, None])
    lower_term = jnp.einsum('rab,rqbc->rqac', jnp.where(lower_mask, own_diag, 0.0), right_factor, precision=HIGHEST)
    upper_term = jnp.einsum('rqab,rqbc->rqac', target_old, jnp.where(upper_mask, their_diag, 0.0), precision=HIGHEST)
    edge_term = jnp.where(lower_tile[:, :, None, None], upper_term, lower_term)
    residue = target_coarse - through - edge_term
    pivots = jnp.maximum(jnp.diagonal(their_diag, axis1=-2, axis2=-1), 1.0)
    scaled = lower_tile[:, :, None, None] | (on_diagonal[:, :, None, None] & lower_mask[None, None])
    return jnp.where(scaled, residue / pivots[:, :, None, :], residue)


def reference(fine_tiles, fine_cols, agg_of, prolong, coarse_cols):
    def coarse_block(block_index):
        start_row = (block_index * FR_DEV).astype(jnp.int32)
        tile_block = lax.dynamic_slice_in_dim(fine_tiles, start_row, FR_DEV, 0).astype(jnp.float32)
        columns = lax.dynamic_slice_in_dim(fine_cols, start_row, FR_DEV, 0)
        own_prolong = lax.dynamic_slice_in_dim(prolong, start_row, FR_DEV, 0).astype(jnp.float32)
        labels = lax.dynamic_slice_in_dim(agg_of, start_row, FR_DEV, 0)
        remote = prolong[columns].astype(jnp.float32)
        carried = jnp.einsum('isab,isbc->isac', tile_block, remote, precision=HIGHEST).astype(jnp.bfloat16)
        carried = lax.optimization_barrier(carried).astype(jnp.float32)
        lifted = jnp.einsum('iba,isbc->isac', own_prolong, carried, precision=HIGHEST)
        targets = agg_of[columns]
        owned_rows = (block_index * COARSE_DEV).astype(jnp.int32) + jnp.arange(COARSE_DEV, dtype=jnp.int32)
        row_pattern = lax.dynamic_slice_in_dim(coarse_cols, (block_index * COARSE_DEV).astype(jnp.int32), COARSE_DEV, 0)
        weights = ((labels[:, None] == owned_rows[None, :])[:, None, :, None] & (row_pattern[None, None, :, :] == targets[:, :, None, None])).astype(jnp.float32)
        return jnp.einsum('isrq,isac->rqac', weights, lifted, precision=HIGHEST)

    blocks = jnp.arange(N_AGG, dtype=jnp.int32)
    coarse = lax.map(coarse_block, blocks).reshape(COARSE, NC, B, B)
    factor = coarse
    for sweep_step in range(SWEEPS):
        def ilu_block(block_index, factor=factor):
            row_base = (block_index * COARSE_DEV).astype(jnp.int32)
            ext_base = jnp.maximum(row_base - COARSE_DEV, 0).astype(jnp.int32)
            ext_full = lax.dynamic_slice_in_dim(factor, ext_base, 2 * COARSE_DEV, 0)
            ext_cols = lax.dynamic_slice_in_dim(coarse_cols, ext_base, 2 * COARSE_DEV, 0)
            row_full = lax.dynamic_slice_in_dim(factor, row_base, COARSE_DEV, 0)
            row_cols = lax.dynamic_slice_in_dim(coarse_cols, row_base, COARSE_DEV, 0)
            row_coarse = lax.dynamic_slice_in_dim(coarse, row_base, COARSE_DEV, 0)
            return relax_rows(row_coarse, row_full, row_cols, row_full, row_cols, ext_full, ext_cols, row_base, ext_base)
        factor = lax.map(ilu_block, blocks).reshape(COARSE, NC, B, B)
    return coarse, factor
```

```python
import functools

import jax
import jax.numpy as jnp
from jax import lax
from jax.experimental import pallas as pl
from jax.experimental.pallas import tpu as pltpu
from jax.sharding import PartitionSpec as P

F32 = jnp.float32
BF16 = jnp.bfloat16
VMEM = pl.BlockSpec(memory_space=pltpu.VMEM)
SMEM = pl.BlockSpec(memory_space=pltpu.SMEM)
ANY = pl.BlockSpec(memory_space=pl.ANY)

ROWS = 12
LIST1 = 16
LIST2 = 160
TILES = 192
KINDS = 240
PLAN = 256
ZERO1 = 64
ZERO2 = 48


def iota(shape, dim):
    return lax.broadcasted_iota(jnp.int32, shape, dim)


def lift_kernel(
    ids, cols, labels, left_labels, right_labels, pattern, tiles, own, left, right, mine, ahead, behind, total, remote
):
    agg, col = ids[0], ids[1]
    total[...] = jnp.zeros_like(total)

    def step(i, carry):
        place = cols[i] - (agg - 1) * 16
        within = place & 15
        side = place >> 4
        target = jnp.where(side == 0, left_labels[within], jnp.where(side == 1, labels[within], right_labels[within]))
        row = labels[i] - agg * 4
        slot = jnp.int32(0)
        for q in range(1, 4):
            slot = jnp.where(pattern[row, q] == target, q, slot)

        @pl.when(side == 0)
        def _():
            remote[...] = left[within]

        @pl.when(side == 1)
        def _():
            remote[...] = own[within]

        @pl.when(side == 2)
        def _():
            remote[...] = right[within]

        carried = jnp.dot(tiles[i], remote[...], preferred_element_type=F32).astype(BF16)
        lifted = lax.dot_general(own[i], carried, (((0,), (0,)), ((), ())), preferred_element_type=F32)
        total[slot, row] += lifted
        return carry

    lax.fori_loop(0, 16, step, 0)
    first = jnp.where(col == 3, 1, col + 1)
    second = jnp.where(col <= 1, 3, col - 1)
    for r in range(4):
        mine[r] = total[col, r]
        ahead[r] = total[first, r].astype(BF16)
        behind[r] = total[second, r].astype(BF16)


def plan_kernel(ids, pattern, near, far, plan, pat, need):
    agg, col = ids[0], ids[1]
    base = (agg - 2) * 4
    for r in range(4):
        for q in range(4):
            pat[4 * r + q] = far[r, q]
            pat[16 + 4 * r + q] = near[r, q]
            pat[32 + 4 * r + q] = pattern[r, q]
    for k in range(32):
        need[k] = 0

    def through(row, index, target, m):
        inner = pat[4 * row + m]
        at = jnp.clip(inner - base, 0, ROWS - 1)
        n = jnp.int32(0)
        for q in range(1, 4):
            n = jnp.where(pat[4 * at + q] == target, q, n)
        valid = (inner < jnp.minimum(index, target)) & (n > 0)
        return at, n, valid

    count = jnp.int32(0)
    for r in range(4):
        row = 8 + r
        index = base + row
        target = pat[4 * row + col]
        lower = target < index
        diagonal = jnp.where(lower, jnp.clip(target - base, 4, ROWS - 1), row) - 4
        need[col * 8 + row - 4] = 1
        need[diagonal] = 1
        for m in range(1, 4):
            at, n, valid = through(row, index, target, m)
            x, y = m * 8 + row - 4, n * 8 + jnp.maximum(at - 4, 0)
            plan[LIST2 + count] = x | (y << 8) | (r << 16)
            count = count + valid.astype(jnp.int32)

            @pl.when(valid)
            def _():
                need[x] = 1
                need[y] = 1

        own = col * 8 + row - 4
        x = jnp.where(lower, own, 40 + row - 4)
        y = jnp.where(target > index, own, 32 + diagonal)
        plan[LIST2 + count] = x | (y << 8) | (r << 16)
        count = count + 1
        kind = jnp.where(lower, 1, jnp.where(target == index, 2, 0))
        plan[KINDS + r] = kind | (diagonal << 8)
    plan[1] = count

    def tile(t, carry):
        @pl.when(need[t] == 1)
        def _():
            products, tiles = plan[0], plan[2]
            row = (t & 7) + 4
            slot = t >> 3
            index = base + row
            target = pat[4 * row + slot]
            lower = target < index
            diagonal = jnp.where(lower, jnp.clip(target - base, 4, ROWS - 1), row) - 4
            for m in range(1, 4):
                at, n, valid = through(row, index, target, m)
                plan[LIST1 + products] = (m * ROWS + row) | ((n * ROWS + at) << 8) | (t << 16)
                products = products + valid.astype(jnp.int32)
            own = slot * ROWS + row
            x = jnp.where(lower, own, 56 + row - 4)
            y = jnp.where(target > index, own, 48 + diagonal)
            plan[LIST1 + products] = x | (y << 8) | (t << 16)
            plan[0] = products + 1
            kind = jnp.where(lower, 1, jnp.where(target == index, 2, 0))
            plan[TILES + tiles] = t | (kind << 8) | (diagonal << 16)
            plan[2] = tiles + 1

        return carry

    plan[0] = 0
    plan[2] = 0
    lax.fori_loop(0, 32, tile, 0)
    plan[LIST1 + plan[0]] = ZERO1 | (ZERO1 << 8) | (32 << 16)


def sweep_kernel(ids, plan, coarse, *refs):
    pieces, (out, first, work, high, low, pivots, pivots_next, sems) = refs[:12], refs[12:]
    col = ids[1]
    width = coarse.shape[-1]
    copies = []
    for k, piece in enumerate(pieces):
        block, shift = k // 4, (0, 3, 1, 2)[k % 4]
        slot = (col + shift) & 3
        start = slot * ROWS + block * 4
        copies.append(pltpu.make_async_copy(piece, first.at[pl.ds(start, 4)], sems.at[k]))
        copies[-1].start()
    first[ZERO1] = jnp.zeros((width, width), BF16)
    lines, columns = iota((width, width), 0), iota((width, width), 1)
    upper, lower, equal = columns > lines, lines > columns, lines == columns

    def reciprocal(tile):
        return 1.0 / jnp.maximum(jnp.sum(jnp.where(equal, tile, 0.0), axis=0, keepdims=True), 1.0)

    for copy in copies:
        copy.wait()

    def prepare(k, carry):
        diagonal = first[4 + k].astype(F32)
        first[48 + k] = jnp.where(upper, diagonal, 0.0).astype(BF16)
        first[56 + k] = jnp.where(lower, diagonal, 0.0).astype(BF16)
        pivots[k] = reciprocal(diagonal)
        return carry

    lax.fori_loop(0, 8, prepare, 0)

    def begin(k, carry):
        t = plan[TILES + k] & 255
        work[t] = first[(t >> 3) * ROWS + (t & 7) + 4].astype(F32)
        return carry

    lax.fori_loop(0, plan[2], begin, 0)

    def multiply(k, carry):
        a, b = plan[LIST1 + 2 * k], plan[LIST1 + 2 * k + 1]
        one = jnp.dot(first[a & 255], first[(a >> 8) & 255], preferred_element_type=F32)
        two = jnp.dot(first[b & 255], first[(b >> 8) & 255], preferred_element_type=F32)
        work[a >> 16] -= one
        work[b >> 16] -= two
        return carry

    lax.fori_loop(0, (plan[0] + 1) >> 1, multiply, 0)

    def scaled(tile, kind, row):
        factor = jnp.where((kind == 1) | ((kind == 2) & lower), row, 1.0)
        return tile * factor

    def split(t, tile):
        top = tile.astype(BF16)
        high[t] = top
        low[t] = (tile - top.astype(F32)).astype(BF16)

    def finish(k, carry):
        entry = plan[TILES + k]
        t, kind, diagonal = entry & 255, (entry >> 8) & 255, entry >> 16
        tile = scaled(work[t], kind, pivots[diagonal])
        split(t, tile)

        @pl.when(t < 8)
        def _():
            split(32 + t, jnp.where(upper, tile, 0.0))
            split(40 + t, jnp.where(lower, tile, 0.0))
            pivots_next[t] = reciprocal(tile)

        return carry

    lax.fori_loop(0, plan[2], finish, 0)
    out[...] = coarse[...]

    def again(k, carry):
        entry = plan[LIST2 + k]
        x, y, r = entry & 255, (entry >> 8) & 255, entry >> 16
        product = jnp.dot(high[x], high[y], preferred_element_type=F32)
        product += jnp.dot(high[x], low[y], preferred_element_type=F32)
        product += jnp.dot(low[x], high[y], preferred_element_type=F32)
        out[r] -= product
        return carry

    lax.fori_loop(0, plan[1], again, 0)
    for r in range(4):
        entry = plan[KINDS + r]
        out[r] = scaled(out[r], entry & 255, pivots_next[entry >> 8])


def along(block, axis, distance, ring=False):
    count = lax.axis_size(axis)
    pairs = [(i, (i + distance) % count) for i in range(count) if ring or 0 <= i + distance < count]
    return lax.ppermute(block, axis, pairs)


def on_device(fine_tiles, fine_cols, agg_of, prolong, coarse_cols):
    width = prolong.shape[-1]
    agg, col = lax.axis_index("agg"), lax.axis_index("col")
    ids = jnp.stack([agg, col]).astype(jnp.int32)
    left, right = along(prolong, "agg", 1), along(prolong, "agg", -1)
    left_labels, right_labels = along(agg_of, "agg", 1), along(agg_of, "agg", -1)
    near, far = along(coarse_cols, "agg", 1), along(coarse_cols, "agg", 2)

    def call(kernel, ins, outs, out_specs, scratch, name):
        return pl.pallas_call(
            kernel,
            out_shape=outs,
            in_specs=ins,
            out_specs=out_specs,
            scratch_shapes=scratch,
            name=name,
            compiler_params=pltpu.CompilerParams(vmem_limit_bytes=60 << 20),
        )

    four = (4, width, width)
    mine, ahead, behind = call(
        lift_kernel,
        [SMEM] * 6 + [VMEM] * 4,
        (jax.ShapeDtypeStruct(four, F32), jax.ShapeDtypeStruct(four, BF16), jax.ShapeDtypeStruct(four, BF16)),
        (VMEM, VMEM, VMEM),
        [pltpu.VMEM((4, *four), F32), pltpu.VMEM((width, width), BF16)],
        "lift",
    )(
        ids,
        fine_cols.reshape(-1),
        agg_of,
        left_labels,
        right_labels,
        coarse_cols,
        fine_tiles.reshape(-1, width, width),
        prolong,
        left,
        right,
    )
    plan = call(
        plan_kernel,
        [SMEM] * 4,
        jax.ShapeDtypeStruct((PLAN,), jnp.int32),
        SMEM,
        [pltpu.SMEM((48,), jnp.int32), pltpu.SMEM((32,), jnp.int32)],
        "plan",
    )(ids, coarse_cols, near, far)

    came_ahead = lax.ppermute(ahead, "col", [(1, 2), (2, 3), (3, 1)])
    came_behind = lax.ppermute(behind, "col", [(1, 3), (2, 1), (3, 2)])
    coarse = mine + came_ahead.astype(F32) + came_behind.astype(F32)
    sent = coarse.astype(BF16)

    def spread(x):
        return [x, along(x, "col", 1, True), along(x, "col", -1, True), along(x, "col", 2, True)]

    here = spread(sent)
    far_sent = along(sent, "agg", 2)
    before = [along(x, "agg", 1) for x in here]
    further = spread(far_sent)
    factor = call(
        sweep_kernel,
        [SMEM] * 2 + [VMEM] + [ANY] * 12,
        jax.ShapeDtypeStruct(four, F32),
        VMEM,
        [
            pltpu.VMEM((65, width, width), BF16),
            pltpu.VMEM((33, width, width), F32),
            pltpu.VMEM((49, width, width), BF16),
            pltpu.VMEM((49, width, width), BF16),
            pltpu.VMEM((8, 1, width), F32),
            pltpu.VMEM((8, 1, width), F32),
            pltpu.SemaphoreType.DMA((12,)),
        ],
        "sweep",
    )(ids, plan, coarse, *further, *before, *here)
    return (coarse[:, None], factor[:, None])


def solution(mesh):
    in_specs = (
        P("agg", "col", None, None),
        P("agg", "col"),
        P("agg"),
        P("agg", None, None),
        P("agg", None),
    )
    out_specs = (P("agg", "col", None, None), P("agg", "col", None, None))
    return jax.shard_map(
        on_device, mesh=mesh, in_specs=in_specs, out_specs=out_specs, check_vma=False
    )
```

```python
import functools

import jax
import jax.numpy as jnp
from jax import lax
from jax.experimental import pallas as pl
from jax.experimental.pallas import tpu as pltpu
from jax.sharding import PartitionSpec as P

F32 = jnp.float32
BF16 = jnp.bfloat16
VMEM = pl.BlockSpec(memory_space=pltpu.VMEM)
SMEM = pl.BlockSpec(memory_space=pltpu.SMEM)
ANY = pl.BlockSpec(memory_space=pl.ANY)

ROWS = 12
LIST1 = 16
LIST2 = 160
TILES = 192
KINDS = 240
CLOSE = 256
DISTANT = 288
PLAN = 320
STEP = 4
ZERO1 = 64
SPARE = 16


def iota(shape, dim):
    return lax.broadcasted_iota(jnp.int32, shape, dim)


def packed_shape(width):
    return (width * width // 128, 128)


def store_packed(ref, tile):
    width, half = tile.shape[0], tile.shape[0] // 2
    ref[:width] = tile[:, :128]
    ref[width:] = jnp.concatenate([tile[:half, 128:], tile[half:, 128:]], axis=1)


def store_unpacked(ref, packed, width):
    half, rest = width // 2, width - 128
    ref[:, :128] = packed[:width]
    ref[:half, 128:] = packed[width:, :rest]
    ref[half:, 128:] = packed[width:, rest:]


def pack_kernel(tiles, packed):
    for i in range(tiles.shape[0]):
        store_packed(packed.at[i], tiles[i])


def entries_of(plan, start, k):
    return [plan[start + STEP * k + u] for u in range(STEP)]


def add_lifted(entries, tiles, turned, remote, total):
    carried = [
        jnp.dot(tiles[e & 255], remote(u, (e >> 8) & 255), preferred_element_type=F32).astype(BF16)
        for u, e in enumerate(entries)
    ]
    lifted = [
        jnp.dot(turned[e & 255], c, preferred_element_type=F32) for e, c in zip(entries, carried)
    ]
    for e, tile in zip(entries, lifted):
        total[e >> 16] += tile


def close_kernel(plan, tiles, own, total, turned):
    total[...] = jnp.zeros_like(total)

    def turn(i, carry):
        turned[i] = own[i].T
        return carry

    lax.fori_loop(0, 16, turn, 0)

    def step(k, carry):
        add_lifted(entries_of(plan, CLOSE, k), tiles, turned, lambda u, place: own[place], total)
        return carry

    lax.fori_loop(0, (plan[3] + STEP - 1) // STEP, step, 0)


def distant_kernel(ids, plan, tiles, turned, left, right, begun, mine, ahead, behind, total, remote):
    col = ids[1]
    total[...] = begun[...]
    width = tiles.shape[-1]

    def step(k, carry):
        entries = entries_of(plan, DISTANT, k)
        for u, e in enumerate(entries):
            place = (e >> 8) & 255

            @pl.when(place < 16)
            def _():
                store_unpacked(remote.at[u], left[place], width)

            @pl.when(place >= 16)
            def _():
                store_unpacked(remote.at[u], right[place - 16], width)

        add_lifted(entries, tiles, turned, lambda u, place: remote[u], total)
        return carry

    lax.fori_loop(0, (plan[4] + STEP - 1) // STEP, step, 0)
    first = jnp.where(col == 3, 1, col + 1)
    second = jnp.where(col <= 1, 3, col - 1)
    for r in range(4):
        mine[r] = total[col * 4 + r]
        store_packed(ahead.at[r], total[first * 4 + r].astype(BF16))
        store_packed(behind.at[r], total[second * 4 + r].astype(BF16))


def combine_kernel(mine, ahead, behind, coarse, sent, wide):
    width = mine.shape[-1]
    for r in range(4):
        store_unpacked(wide, ahead[r].astype(F32) + behind[r].astype(F32), width)
        tile = mine[r] + wide[...]
        coarse[r] = tile
        store_packed(sent.at[r], tile.astype(BF16))


def plan_kernel(ids, cols, labels, pattern, near, right_labels, far, plan, pat, need):
    agg, col = ids[0], ids[1]
    base = (agg - 2) * 4
    for r in range(4):
        for q in range(4):
            pat[4 * r + q] = far[r, q]
            pat[16 + 4 * r + q] = near[16 + 4 * r + q]
            pat[32 + 4 * r + q] = pattern[r, q]
    for k in range(32):
        need[k] = 0

    def fine(i, carry):
        close, distant = carry
        place = cols[i] - (agg - 1) * 16
        within = place & 15
        side = place >> 4
        target = jnp.where(side == 0, near[within], jnp.where(side == 1, labels[within], right_labels[within]))
        row = labels[i] - agg * 4
        slot = jnp.int32(0)
        for q in range(1, 4):
            slot = jnp.where(pat[32 + 4 * row + q] == target, q, slot)
        entry = i | ((slot * 4 + row) << 16)
        plan[CLOSE + close] = entry | (within << 8)
        plan[DISTANT + distant] = entry | ((within + jnp.where(side == 0, 0, 16)) << 8)
        here = (side == 1).astype(jnp.int32)
        return close + here, distant + 1 - here

    close, distant = lax.fori_loop(0, 16, fine, (jnp.int32(0), jnp.int32(0)))
    plan[3] = close
    plan[4] = distant
    for u in range(STEP - 1):
        plan[CLOSE + close + u] = SPARE << 16
        plan[DISTANT + distant + u] = SPARE << 16

    def through(row, index, target, m):
        inner = pat[4 * row + m]
        at = jnp.clip(inner - base, 0, ROWS - 1)
        n = jnp.int32(0)
        for q in range(1, 4):
            n = jnp.where(pat[4 * at + q] == target, q, n)
        valid = (inner < jnp.minimum(index, target)) & (n > 0)
        return at, n, valid

    count = jnp.int32(0)
    for r in range(4):
        row = 8 + r
        index = base + row
        target = pat[4 * row + col]
        lower = target < index
        diagonal = jnp.where(lower, jnp.clip(target - base, 4, ROWS - 1), row) - 4
        need[col * 8 + row - 4] = 1
        need[diagonal] = 1
        for m in range(1, 4):
            at, n, valid = through(row, index, target, m)
            x, y = m * 8 + row - 4, n * 8 + jnp.maximum(at - 4, 0)
            plan[LIST2 + count] = x | (y << 8) | (r << 16)
            count = count + valid.astype(jnp.int32)

            @pl.when(valid)
            def _():
                need[x] = 1
                need[y] = 1

        own = col * 8 + row - 4
        x = jnp.where(lower, own, 40 + row - 4)
        y = jnp.where(target > index, own, 32 + diagonal)
        plan[LIST2 + count] = x | (y << 8) | (r << 16)
        count = count + 1
        kind = jnp.where(lower, 1, jnp.where(target == index, 2, 0))
        plan[KINDS + r] = kind | (diagonal << 8)
    plan[1] = count

    def tile(t, carry):
        @pl.when(need[t] == 1)
        def _():
            products, tiles = plan[0], plan[2]
            row = (t & 7) + 4
            slot = t >> 3
            index = base + row
            target = pat[4 * row + slot]
            lower = target < index
            diagonal = jnp.where(lower, jnp.clip(target - base, 4, ROWS - 1), row) - 4
            for m in range(1, 4):
                at, n, valid = through(row, index, target, m)
                plan[LIST1 + products] = (m * ROWS + row) | ((n * ROWS + at) << 8) | (t << 16)
                products = products + valid.astype(jnp.int32)
            own = slot * ROWS + row
            x = jnp.where(lower, own, 56 + row - 4)
            y = jnp.where(target > index, own, 48 + diagonal)
            plan[LIST1 + products] = x | (y << 8) | (t << 16)
            plan[0] = products + 1
            kind = jnp.where(lower, 1, jnp.where(target == index, 2, 0))
            plan[TILES + tiles] = t | (kind << 8) | (diagonal << 16)
            plan[2] = tiles + 1

        return carry

    plan[0] = 0
    plan[2] = 0
    lax.fori_loop(0, 32, tile, 0)
    for u in range(STEP - 1):
        plan[LIST1 + plan[0] + u] = ZERO1 | (ZERO1 << 8) | (32 << 16)


def sweep_kernel(ids, plan, coarse, *refs):
    pieces, (out, arrived, first, work, high, low, pivots, pivots_next, sems) = refs[:12], refs[12:]
    col = ids[1]
    width = coarse.shape[-1]
    copies = []
    for k, piece in enumerate(pieces):
        copies.append(pltpu.make_async_copy(piece, arrived.at[pl.ds(4 * k, 4)], sems.at[k]))
        copies[-1].start()
    first[ZERO1] = jnp.zeros((width, width), BF16)
    lines, columns = iota((width, width), 0), iota((width, width), 1)
    upper, lower, equal = columns > lines, lines > columns, lines == columns

    def reciprocal(tile):
        return 1.0 / jnp.maximum(jnp.sum(jnp.where(equal, tile, 0.0), axis=0, keepdims=True), 1.0)

    for k, copy in enumerate(copies):
        copy.wait()
        start = ((col + (0, 3, 1, 2)[k % 4]) & 3) * ROWS + k // 4 * 4
        for r in range(4):
            store_unpacked(first.at[start + r], arrived[4 * k + r], width)

    def prepare(k, carry):
        diagonal = first[4 + k].astype(F32)
        first[48 + k] = jnp.where(upper, diagonal, 0.0).astype(BF16)
        first[56 + k] = jnp.where(lower, diagonal, 0.0).astype(BF16)
        pivots[k] = reciprocal(diagonal)
        return carry

    lax.fori_loop(0, 8, prepare, 0)

    def begin(k, carry):
        t = plan[TILES + k] & 255
        work[t] = first[(t >> 3) * ROWS + (t & 7) + 4].astype(F32)
        return carry

    lax.fori_loop(0, plan[2], begin, 0)

    def multiply(k, carry):
        entries = entries_of(plan, LIST1, k)
        products = [jnp.dot(first[e & 255], first[(e >> 8) & 255], preferred_element_type=F32) for e in entries]
        for e, product in zip(entries, products):
            work[e >> 16] -= product
        return carry

    lax.fori_loop(0, (plan[0] + STEP - 1) // STEP, multiply, 0)

    def scaled(tile, kind, row):
        factor = jnp.where((kind == 1) | ((kind == 2) & lower), row, 1.0)
        return tile * factor

    def split(t, tile):
        top = tile.astype(BF16)
        high[t] = top
        low[t] = (tile - top.astype(F32)).astype(BF16)

    def finish(k, carry):
        entry = plan[TILES + k]
        t, kind, diagonal = entry & 255, (entry >> 8) & 255, entry >> 16
        tile = scaled(work[t], kind, pivots[diagonal])
        split(t, tile)

        @pl.when(t < 8)
        def _():
            split(32 + t, jnp.where(upper, tile, 0.0))
            split(40 + t, jnp.where(lower, tile, 0.0))
            pivots_next[t] = reciprocal(tile)

        return carry

    lax.fori_loop(0, plan[2], finish, 0)
    out[...] = coarse[...]

    def again(k, carry):
        entry = plan[LIST2 + k]
        x, y, r = entry & 255, (entry >> 8) & 255, entry >> 16
        product = jnp.dot(high[x], high[y], preferred_element_type=F32)
        product += jnp.dot(high[x], low[y], preferred_element_type=F32)
        product += jnp.dot(low[x], high[y], preferred_element_type=F32)
        out[r] -= product
        return carry

    lax.fori_loop(0, plan[1], again, 0)
    for r in range(4):
        entry = plan[KINDS + r]
        out[r] = scaled(out[r], entry & 255, pivots_next[entry >> 8])


def along(block, axis, distance, ring=False, sources=None):
    count = lax.axis_size(axis)
    pairs = [(i, (i + distance) % count) for i in range(count) if ring or 0 <= i + distance < count]
    return lax.ppermute(block, axis, [pair for pair in pairs if sources is None or pair[0] in sources])


def on_device(fine_tiles, fine_cols, agg_of, prolong, coarse_cols):
    rows, width = prolong.shape[0], prolong.shape[-1]
    agg, col = lax.axis_index("agg"), lax.axis_index("col")
    ids = jnp.stack([agg, col]).astype(jnp.int32)
    packed = packed_shape(width)
    four, four_packed = (4, width, width), (4, *packed)

    def array(shape, dtype):
        return jax.ShapeDtypeStruct(shape, dtype)

    def call(kernel, ins, outs, out_specs, scratch, name, mebibytes):
        return pl.pallas_call(
            kernel,
            out_shape=outs,
            in_specs=ins,
            out_specs=out_specs,
            scratch_shapes=scratch,
            name=name,
            compiler_params=pltpu.CompilerParams(vmem_limit_bytes=mebibytes << 20),
        )

    about = jnp.concatenate([agg_of, coarse_cols.reshape(-1)])
    near, far = along(about, "agg", 1), along(coarse_cols, "agg", 2)
    right_labels = along(agg_of, "agg", -1)
    halo = call(pack_kernel, [VMEM], array((rows, *packed), BF16), VMEM, [], "pack", 10)(prolong)
    left, right = along(halo, "agg", 1), along(halo, "agg", -1)

    plan = call(
        plan_kernel,
        [SMEM] * 7,
        array((PLAN,), jnp.int32),
        SMEM,
        [pltpu.SMEM((48,), jnp.int32), pltpu.SMEM((32,), jnp.int32)],
        "plan",
        4,
    )(ids, fine_cols.reshape(-1), agg_of, coarse_cols, near, right_labels, far)
    tiles = fine_tiles.reshape(rows, width, width)
    total, turned = call(
        close_kernel,
        [SMEM, VMEM, VMEM],
        (array((SPARE + 1, width, width), F32), array((rows, width, width), BF16)),
        (VMEM, VMEM),
        [],
        "close",
        14,
    )(plan, tiles, prolong)
    mine, ahead, behind = call(
        distant_kernel,
        [SMEM] * 2 + [VMEM] * 5,
        (array(four, F32), array(four_packed, BF16), array(four_packed, BF16)),
        (VMEM,) * 3,
        [pltpu.VMEM((SPARE + 1, width, width), F32), pltpu.VMEM((STEP, width, width), BF16)],
        "distant",
        22,
    )(ids, plan, tiles, turned, left, right, total)

    came_ahead = lax.ppermute(ahead, "col", [(1, 2), (2, 3), (3, 1)])
    came_behind = lax.ppermute(behind, "col", [(1, 3), (2, 1), (3, 2)])
    coarse, sent = call(
        combine_kernel,
        [VMEM] * 3,
        (array(four, F32), array(four_packed, BF16)),
        (VMEM, VMEM),
        [pltpu.VMEM((width, width), F32)],
        "combine",
        8,
    )(mine, came_ahead, came_behind)

    here = [sent] + [along(sent, "col", d, True) for d in (1, -1, 2)]
    before = [along(x, "agg", 1) for x in here]
    others = (1, 2, 3)
    second = along(before[0], "agg", 1)
    further = [second] + [along(second, "col", d, True, others) for d in (1, -1)] + [along(before[3], "agg", 1)]
    factor = call(
        sweep_kernel,
        [SMEM] * 2 + [VMEM] + [ANY] * 12,
        array(four, F32),
        VMEM,
        [
            pltpu.VMEM((48, *packed), BF16),
            pltpu.VMEM((65, width, width), BF16),
            pltpu.VMEM((33, width, width), F32),
            pltpu.VMEM((49, width, width), BF16),
            pltpu.VMEM((49, width, width), BF16),
            pltpu.VMEM((8, 1, width), F32),
            pltpu.VMEM((8, 1, width), F32),
            pltpu.SemaphoreType.DMA((12,)),
        ],
        "sweep",
        34,
    )(ids, plan, coarse, *further, *before, *here)
    return (coarse[:, None], factor[:, None])


def solution(mesh):
    in_specs = (
        P("agg", "col", None, None),
        P("agg", "col"),
        P("agg"),
        P("agg", None, None),
        P("agg", None),
    )
    out_specs = (P("agg", "col", None, None), P("agg", "col", None, None))
    return jax.shard_map(
        on_device, mesh=mesh, in_specs=in_specs, out_specs=out_specs, check_vma=False
    )
```

```python
import functools

import jax
import jax.numpy as jnp
from jax import lax
from jax.experimental import pallas as pl
from jax.experimental.pallas import tpu as pltpu
from jax.sharding import PartitionSpec as P

F32 = jnp.float32
BF16 = jnp.bfloat16
VMEM = pl.BlockSpec(memory_space=pltpu.VMEM)
SMEM = pl.BlockSpec(memory_space=pltpu.SMEM)
ANY = pl.BlockSpec(memory_space=pl.ANY)

ROWS = 12
LIST1 = 16
LIST2 = 160
TILES = 192
KINDS = 240
PLAN = 256
STEP = 4
ZERO1 = 64
SPARE = 16


def iota(shape, dim):
    return lax.broadcasted_iota(jnp.int32, shape, dim)


def packed_shape(width):
    return (width * width // 128, 128)


def store_packed(ref, tile):
    width, half = tile.shape[0], tile.shape[0] // 2
    ref[:width] = tile[:, :128]
    ref[width:] = jnp.concatenate([tile[:half, 128:], tile[half:, 128:]], axis=1)


def store_unpacked(ref, packed, width):
    half, rest = width // 2, width - 128
    ref[:, :128] = packed[:width]
    ref[:half, 128:] = packed[width:, :rest]
    ref[half:, 128:] = packed[width:, rest:]


def pack_kernel(labels, pattern, tiles, packed):
    count, size = tiles.shape[0], tiles.shape[1] * tiles.shape[2] // 128
    line, lane = iota((16, 128), 0), iota((16, 128), 1)
    about = jnp.zeros((16, 128), F32)
    for i in range(count):
        about = jnp.where((line == 0) & (lane == i), (labels[i] & 3).astype(F32), about)
    for r in range(4):
        for q in range(1, 4):
            offset = pattern[r, q] - pattern[r, 0]
            about = jnp.where((line == 1) & (lane == 4 * r + q), offset.astype(F32), about)
    packed[count * size :] = about.astype(BF16)
    for i in range(count):
        store_packed(packed.at[pl.ds(i * size, size)], tiles[i])


def entries_of(plan, start, k):
    return [plan[start + STEP * k + u] for u in range(STEP)]


def add_lifted(entries, tiles, turned, remote, total):
    carried = [
        jnp.dot(tiles[e & 255], remote(u, (e >> 8) & 255), preferred_element_type=F32).astype(BF16)
        for u, e in enumerate(entries)
    ]
    lifted = [
        jnp.dot(turned[e & 255], c, preferred_element_type=F32) for e, c in zip(entries, carried)
    ]
    for e, tile in zip(entries, lifted):
        total[e >> 16] += tile


def slot_of(pattern, row, target):
    slot = jnp.int32(0)
    for q in range(1, 4):
        slot = jnp.where(pattern[row, q] == target, q, slot)
    return slot


def close_kernel(ids, cols, labels, pattern, tiles, own, total, turned, work):
    agg = ids[0]

    def note(i, count):
        place = cols[i] - agg * 16
        row = labels[i] & 3
        slot = slot_of(pattern, row, labels[place & 15])
        work[count] = i | ((place & 15) << 8) | ((slot * 4 + row) << 16)
        return count + (place >> 4 == 0).astype(jnp.int32)

    count = lax.fori_loop(0, 16, note, jnp.int32(0))
    for u in range(STEP - 1):
        work[count + u] = SPARE << 16
    total[...] = jnp.zeros_like(total)

    def turn(i, carry):
        turned[i] = own[i].T
        return carry

    lax.fori_loop(0, 16, turn, 0)

    def step(k, carry):
        add_lifted(entries_of(work, 0, k), tiles, turned, lambda u, place: own[place], total)
        return carry

    lax.fori_loop(0, (count + STEP - 1) // STEP, step, 0)


def distant_kernel(ids, cols, labels, pattern, tiles, turned, left, right, begun, *refs):
    mine, ahead, behind, near, total, remote, seen, about, work, sem = refs
    agg, col = ids[0], ids[1]
    width = tiles.shape[-1]
    size = width * width // 128
    end = 16 * size
    seen[:16] = left[end:].astype(F32).astype(jnp.int32)
    seen[16:] = right[end:].astype(F32).astype(jnp.int32)
    copy = pltpu.make_async_copy(seen, about, sem)
    copy.start()
    total[...] = begun[...]
    copy.wait()

    def note(i, count):
        place = cols[i] - (agg - 1) * 16
        side, within = place >> 4, place & 15
        target = jnp.where(side == 0, about[0, within] + 4 * agg - 4, about[16, within] + 4 * agg + 4)
        row = labels[i] & 3
        slot = slot_of(pattern, row, target)
        work[count] = i | ((within + jnp.where(side == 0, 0, 16)) << 8) | ((slot * 4 + row) << 16)
        return count + (side != 1).astype(jnp.int32)

    count = lax.fori_loop(0, 16, note, jnp.int32(0))
    for u in range(STEP - 1):
        work[count + u] = SPARE << 16
    for k in range(16):
        near[k] = 4 * agg - 4 + k // 4 + about[1, k]

    def step(k, carry):
        entries = entries_of(work, 0, k)
        for u, e in enumerate(entries):
            place = (e >> 8) & 255
            start = pl.multiple_of((place & 15) * size, 16)

            @pl.when(place < 16)
            def _():
                store_unpacked(remote.at[u], left[pl.ds(start, size)], width)

            @pl.when(place >= 16)
            def _():
                store_unpacked(remote.at[u], right[pl.ds(start, size)], width)

        add_lifted(entries, tiles, turned, lambda u, place: remote[u], total)
        return carry

    lax.fori_loop(0, (count + STEP - 1) // STEP, step, 0)
    first = jnp.where(col == 3, 1, col + 1)
    second = jnp.where(col <= 1, 3, col - 1)
    for r in range(4):
        mine[r] = total[col * 4 + r]
        store_packed(ahead.at[r], total[first * 4 + r].astype(BF16))
        store_packed(behind.at[r], total[second * 4 + r].astype(BF16))


def combine_kernel(plan, mine, ahead, behind, coarse, sent, kept, wide):
    width = mine.shape[-1]
    for r in range(4):
        store_unpacked(wide, ahead[r].astype(F32) + behind[r].astype(F32), width)
        tile = mine[r] + wide[...]
        coarse[r] = tile
        kept[r] = tile
        store_packed(sent.at[r], tile.astype(BF16))


def plan_kernel(ids, pattern, near, far, plan, pat, need):
    agg, col = ids[0], ids[1]
    base = (agg - 2) * 4
    for k in range(16):
        pat[k] = far[k]
        pat[16 + k] = near[k]
        pat[32 + k] = pattern[k // 4, k % 4]
    for k in range(32):
        need[k] = 0

    def through(row, index, target, m):
        inner = pat[4 * row + m]
        at = jnp.clip(inner - base, 0, ROWS - 1)
        n = jnp.int32(0)
        for q in range(1, 4):
            n = jnp.where(pat[4 * at + q] == target, q, n)
        valid = (inner < jnp.minimum(index, target)) & (n > 0)
        return at, n, valid

    count = jnp.int32(0)
    for r in range(4):
        row = 8 + r
        index = base + row
        target = pat[4 * row + col]
        lower = target < index
        diagonal = jnp.where(lower, jnp.clip(target - base, 4, ROWS - 1), row) - 4
        need[col * 8 + row - 4] = 1
        need[diagonal] = 1
        for m in range(1, 4):
            at, n, valid = through(row, index, target, m)
            x, y = m * 8 + row - 4, n * 8 + jnp.maximum(at - 4, 0)
            plan[LIST2 + count] = x | (y << 8) | (r << 16)
            count = count + valid.astype(jnp.int32)

            @pl.when(valid)
            def _():
                need[x] = 1
                need[y] = 1

        own = col * 8 + row - 4
        x = jnp.where(lower, own, 40 + row - 4)
        y = jnp.where(target > index, own, 32 + diagonal)
        plan[LIST2 + count] = x | (y << 8) | (r << 16)
        count = count + 1
        kind = jnp.where(lower, 1, jnp.where(target == index, 2, 0))
        plan[KINDS + r] = kind | (diagonal << 8)
    plan[1] = count

    def tile(t, carry):
        @pl.when(need[t] == 1)
        def _():
            products, tiles = plan[0], plan[2]
            row = (t & 7) + 4
            slot = t >> 3
            index = base + row
            target = pat[4 * row + slot]
            lower = target < index
            diagonal = jnp.where(lower, jnp.clip(target - base, 4, ROWS - 1), row) - 4
            for m in range(1, 4):
                at, n, valid = through(row, index, target, m)
                plan[LIST1 + products] = (m * ROWS + row) | ((n * ROWS + at) << 8) | (t << 16)
                products = products + valid.astype(jnp.int32)
            own = slot * ROWS + row
            x = jnp.where(lower, own, 56 + row - 4)
            y = jnp.where(target > index, own, 48 + diagonal)
            plan[LIST1 + products] = x | (y << 8) | (t << 16)
            plan[0] = products + 1
            kind = jnp.where(lower, 1, jnp.where(target == index, 2, 0))
            plan[TILES + tiles] = t | (kind << 8) | (diagonal << 16)
            plan[2] = tiles + 1

        return carry

    plan[0] = 0
    plan[2] = 0
    lax.fori_loop(0, 32, tile, 0)
    for u in range(STEP - 1):
        plan[LIST1 + plan[0] + u] = ZERO1 | (ZERO1 << 8) | (32 << 16)


def sweep_kernel(ids, plan, coarse, *refs):
    pieces, (out, arrived, first, work, high, low, pivots, pivots_next, sems) = refs[:12], refs[12:]
    col = ids[1]
    width = coarse.shape[-1]
    copies = []
    for k, piece in enumerate(pieces):
        copies.append(pltpu.make_async_copy(piece, arrived.at[pl.ds(4 * k, 4)], sems.at[k]))
        copies[-1].start()
    first[ZERO1] = jnp.zeros((width, width), BF16)
    lines, columns = iota((width, width), 0), iota((width, width), 1)
    upper, lower, equal = columns > lines, lines > columns, lines == columns

    def reciprocal(tile):
        return 1.0 / jnp.maximum(jnp.sum(jnp.where(equal, tile, 0.0), axis=0, keepdims=True), 1.0)

    for k, copy in enumerate(copies):
        copy.wait()
        start = ((col + (0, 3, 1, 2)[k % 4]) & 3) * ROWS + k // 4 * 4
        for r in range(4):
            store_unpacked(first.at[start + r], arrived[4 * k + r], width)

    def prepare(k, carry):
        diagonal = first[4 + k].astype(F32)
        first[48 + k] = jnp.where(upper, diagonal, 0.0).astype(BF16)
        first[56 + k] = jnp.where(lower, diagonal, 0.0).astype(BF16)
        pivots[k] = reciprocal(diagonal)
        return carry

    lax.fori_loop(0, 8, prepare, 0)

    def begin(k, carry):
        t = plan[TILES + k] & 255
        work[t] = first[(t >> 3) * ROWS + (t & 7) + 4].astype(F32)
        return carry

    lax.fori_loop(0, plan[2], begin, 0)

    def multiply(k, carry):
        entries = entries_of(plan, LIST1, k)
        products = [jnp.dot(first[e & 255], first[(e >> 8) & 255], preferred_element_type=F32) for e in entries]
        for e, product in zip(entries, products):
            work[e >> 16] -= product
        return carry

    lax.fori_loop(0, (plan[0] + STEP - 1) // STEP, multiply, 0)

    def scaled(tile, kind, row):
        factor = jnp.where((kind == 1) | ((kind == 2) & lower), row, 1.0)
        return tile * factor

    def split(t, tile):
        top = tile.astype(BF16)
        high[t] = top
        low[t] = (tile - top.astype(F32)).astype(BF16)

    def finish(k, carry):
        entry = plan[TILES + k]
        t, kind, diagonal = entry & 255, (entry >> 8) & 255, entry >> 16
        tile = scaled(work[t], kind, pivots[diagonal])
        split(t, tile)

        @pl.when(t < 8)
        def _():
            split(32 + t, jnp.where(upper, tile, 0.0))
            split(40 + t, jnp.where(lower, tile, 0.0))
            pivots_next[t] = reciprocal(tile)

        return carry

    lax.fori_loop(0, plan[2], finish, 0)
    out[...] = coarse[...]

    def again(k, carry):
        entry = plan[LIST2 + k]
        x, y, r = entry & 255, (entry >> 8) & 255, entry >> 16
        product = jnp.dot(high[x], high[y], preferred_element_type=F32)
        product += jnp.dot(high[x], low[y], preferred_element_type=F32)
        product += jnp.dot(low[x], high[y], preferred_element_type=F32)
        out[r] -= product
        return carry

    lax.fori_loop(0, plan[1], again, 0)
    for r in range(4):
        entry = plan[KINDS + r]
        out[r] = scaled(out[r], entry & 255, pivots_next[entry >> 8])


def along(block, axis, distance, ring=False, sources=None):
    count = lax.axis_size(axis)
    pairs = [(i, (i + distance) % count) for i in range(count) if ring or 0 <= i + distance < count]
    return lax.ppermute(block, axis, [pair for pair in pairs if sources is None or pair[0] in sources])


def on_device(fine_tiles, fine_cols, agg_of, prolong, coarse_cols):
    rows, width = prolong.shape[0], prolong.shape[-1]
    agg, col = lax.axis_index("agg"), lax.axis_index("col")
    ids = jnp.stack([agg, col]).astype(jnp.int32)
    packed = packed_shape(width)
    four, four_packed = (4, width, width), (4, *packed)

    def array(shape, dtype):
        return jax.ShapeDtypeStruct(shape, dtype)

    def call(kernel, ins, outs, out_specs, scratch, name, mebibytes):
        return pl.pallas_call(
            kernel,
            out_shape=outs,
            in_specs=ins,
            out_specs=out_specs,
            scratch_shapes=scratch,
            name=name,
            compiler_params=pltpu.CompilerParams(vmem_limit_bytes=mebibytes << 20),
        )

    cols = fine_cols.reshape(-1)
    tiles = fine_tiles.reshape(rows, width, width)
    halo_shape = (rows * packed[0] + 16, 128)
    halo = call(pack_kernel, [SMEM] * 2 + [VMEM], array(halo_shape, BF16), VMEM, [], "pack", 10)(
        agg_of, coarse_cols, prolong
    )
    left, right = along(halo, "agg", 1), along(halo, "agg", -1)
    total, turned = call(
        close_kernel,
        [SMEM] * 4 + [VMEM] * 2,
        (array((SPARE + 1, width, width), F32), array((rows, width, width), BF16)),
        (VMEM, VMEM),
        [pltpu.SMEM((20,), jnp.int32)],
        "close",
        14,
    )(ids, cols, agg_of, coarse_cols, tiles, prolong)
    mine, ahead, behind, near = call(
        distant_kernel,
        [SMEM] * 4 + [VMEM] * 5,
        (array(four, F32), array(four_packed, BF16), array(four_packed, BF16), array((16,), jnp.int32)),
        (VMEM, VMEM, VMEM, SMEM),
        [
            pltpu.VMEM((SPARE + 1, width, width), F32),
            pltpu.VMEM((STEP, width, width), BF16),
            pltpu.VMEM((32, 128), jnp.int32),
            pltpu.SMEM((32, 128), jnp.int32),
            pltpu.SMEM((20,), jnp.int32),
            pltpu.SemaphoreType.DMA,
        ],
        "distant",
        22,
    )(ids, cols, agg_of, coarse_cols, tiles, turned, left, right, total)

    came_ahead = lax.ppermute(ahead, "col", [(1, 2), (2, 3), (3, 1)])
    came_behind = lax.ppermute(behind, "col", [(1, 3), (2, 1), (3, 2)])
    far = along(near, "agg", 1)
    plan = call(
        plan_kernel,
        [SMEM] * 4,
        array((PLAN,), jnp.int32),
        SMEM,
        [pltpu.SMEM((48,), jnp.int32), pltpu.SMEM((32,), jnp.int32)],
        "plan",
        4,
    )(ids, coarse_cols, near, far)
    coarse, sent, kept = call(
        combine_kernel,
        [SMEM] + [VMEM] * 3,
        (array(four, F32), array(four_packed, BF16), array(four, F32)),
        (VMEM, VMEM, VMEM),
        [pltpu.VMEM((width, width), F32)],
        "combine",
        8,
    )(plan, mine, came_ahead, came_behind)

    here = [sent] + [along(sent, "col", d, True) for d in (1, -1, 2)]
    before = [along(x, "agg", 1) for x in here]
    others = (1, 2, 3)
    second = along(before[0], "agg", 1)
    further = [second] + [along(second, "col", d, True, others) for d in (1, -1)] + [along(before[3], "agg", 1)]
    factor = call(
        sweep_kernel,
        [SMEM] * 2 + [VMEM] + [ANY] * 12,
        array(four, F32),
        VMEM,
        [
            pltpu.VMEM((48, *packed), BF16),
            pltpu.VMEM((65, width, width), BF16),
            pltpu.VMEM((33, width, width), F32),
            pltpu.VMEM((49, width, width), BF16),
            pltpu.VMEM((49, width, width), BF16),
            pltpu.VMEM((8, 1, width), F32),
            pltpu.VMEM((8, 1, width), F32),
            pltpu.SemaphoreType.DMA((12,)),
        ],
        "sweep",
        34,
    )(ids, plan, kept, *further, *before, *here)
    return (coarse[:, None], factor[:, None])


def solution(mesh):
    in_specs = (
        P("agg", "col", None, None),
        P("agg", "col"),
        P("agg"),
        P("agg", None, None),
        P("agg", None),
    )
    out_specs = (P("agg", "col", None, None), P("agg", "col", None, None))
    return jax.shard_map(
        on_device, mesh=mesh, in_specs=in_specs, out_specs=out_specs, check_vma=False
    )
```

```python
import functools

import jax
import jax.numpy as jnp
from jax import lax
from jax.experimental import pallas as pl
from jax.experimental.pallas import tpu as pltpu
from jax.sharding import PartitionSpec as P

F32 = jnp.float32
BF16 = jnp.bfloat16
VMEM = pl.BlockSpec(memory_space=pltpu.VMEM)
SMEM = pl.BlockSpec(memory_space=pltpu.SMEM)
ANY = pl.BlockSpec(memory_space=pl.ANY)

ROWS = 12
LIST1 = 16
LIST2 = 160
TILES = 192
KINDS = 240
PLAN = 256
STEP = 4
ZERO1 = 64
SPARE = 16


def iota(shape, dim):
    return lax.broadcasted_iota(jnp.int32, shape, dim)


def packed_shape(width):
    return (width * width // 128, 128)


def store_packed(ref, tile):
    width, half = tile.shape[0], tile.shape[0] // 2
    ref[:width] = tile[:, :128]
    ref[width:] = jnp.concatenate([tile[:half, 128:], tile[half:, 128:]], axis=1)


def store_unpacked(ref, packed, width):
    half, rest = width // 2, width - 128
    ref[:, :128] = packed[:width]
    ref[:half, 128:] = packed[width:, :rest]
    ref[half:, 128:] = packed[width:, rest:]


def pack_kernel(labels, pattern, tiles, packed):
    count, size = tiles.shape[0], tiles.shape[1] * tiles.shape[2] // 128
    line, lane = iota((16, 128), 0), iota((16, 128), 1)
    about = jnp.zeros((16, 128), F32)
    for i in range(count):
        about = jnp.where((line == 0) & (lane == i), (labels[i] & 3).astype(F32), about)
    for r in range(4):
        for q in range(1, 4):
            offset = pattern[r, q] - pattern[r, 0]
            about = jnp.where((line == 1) & (lane == 4 * r + q), offset.astype(F32), about)
    packed[count * size :] = about.astype(BF16)
    for i in range(count):
        store_packed(packed.at[pl.ds(i * size, size)], tiles[i])


def entries_of(plan, start, k):
    return [plan[start + STEP * k + u] for u in range(STEP)]


def add_lifted(entries, tiles, turned, remote, total):
    carried = [
        jnp.dot(tiles[e & 255], remote(u, (e >> 8) & 255), preferred_element_type=F32).astype(BF16)
        for u, e in enumerate(entries)
    ]
    lifted = [
        jnp.dot(turned[e & 255], c, preferred_element_type=F32) for e, c in zip(entries, carried)
    ]
    for e, tile in zip(entries, lifted):
        total[e >> 16] += tile


def slot_of(pattern, row, target):
    slot = jnp.int32(0)
    for q in range(1, 4):
        slot = jnp.where(pattern[row, q] == target, q, slot)
    return slot


def close_kernel(ids, cols, labels, pattern, tiles, own, total, turned, work):
    agg = ids[0]

    def note(i, count):
        place = cols[i] - agg * 16
        row = labels[i] & 3
        slot = slot_of(pattern, row, labels[place & 15])
        work[count] = i | ((place & 15) << 8) | ((slot * 4 + row) << 16)
        return count + (place >> 4 == 0).astype(jnp.int32)

    count = lax.fori_loop(0, 16, note, jnp.int32(0))
    for u in range(STEP - 1):
        work[count + u] = SPARE << 16
    total[...] = jnp.zeros_like(total)

    def turn(i, carry):
        turned[i] = own[i].T
        return carry

    lax.fori_loop(0, 16, turn, 0)

    def step(k, carry):
        add_lifted(entries_of(work, 0, k), tiles, turned, lambda u, place: own[place], total)
        return carry

    lax.fori_loop(0, (count + STEP - 1) // STEP, step, 0)


def distant_kernel(ids, cols, labels, pattern, tiles, turned, left, right, begun, *refs):
    mine, ahead, behind, near, total, remote, seen, about, work, sem = refs
    agg, col = ids[0], ids[1]
    width = tiles.shape[-1]
    size = width * width // 128
    end = 16 * size
    seen[:16] = left[end:].astype(F32).astype(jnp.int32)
    seen[16:] = right[end:].astype(F32).astype(jnp.int32)
    copy = pltpu.make_async_copy(seen, about, sem)
    copy.start()
    total[...] = begun[...]
    copy.wait()

    def note(i, count):
        place = cols[i] - (agg - 1) * 16
        side, within = place >> 4, place & 15
        target = jnp.where(side == 0, about[0, within] + 4 * agg - 4, about[16, within] + 4 * agg + 4)
        row = labels[i] & 3
        slot = slot_of(pattern, row, target)
        work[count] = i | ((within + jnp.where(side == 0, 0, 16)) << 8) | ((slot * 4 + row) << 16)
        return count + (side != 1).astype(jnp.int32)

    count = lax.fori_loop(0, 16, note, jnp.int32(0))
    for u in range(STEP - 1):
        work[count + u] = SPARE << 16
    for k in range(16):
        near[k] = 4 * agg - 4 + k // 4 + about[1, k]

    def step(k, carry):
        entries = entries_of(work, 0, k)
        for u, e in enumerate(entries):
            place = (e >> 8) & 255
            start = pl.multiple_of((place & 15) * size, 16)

            @pl.when(place < 16)
            def _():
                store_unpacked(remote.at[u], left[pl.ds(start, size)], width)

            @pl.when(place >= 16)
            def _():
                store_unpacked(remote.at[u], right[pl.ds(start, size)], width)

        add_lifted(entries, tiles, turned, lambda u, place: remote[u], total)
        return carry

    lax.fori_loop(0, (count + STEP - 1) // STEP, step, 0)
    first = jnp.where(col == 3, 1, col + 1)
    second = jnp.where(col <= 1, 3, col - 1)
    for r in range(4):
        mine[r] = total[col * 4 + r]
        store_packed(ahead.at[r], total[first * 4 + r].astype(BF16))
        store_packed(behind.at[r], total[second * 4 + r].astype(BF16))


def combine_kernel(plan, mine, ahead, behind, coarse, sent, kept, wide):
    width = mine.shape[-1]
    for r in range(4):
        store_unpacked(wide, ahead[r].astype(F32) + behind[r].astype(F32), width)
        tile = mine[r] + wide[...]
        coarse[r] = tile
        kept[r] = tile
        store_packed(sent.at[r], tile.astype(BF16))


def plan_kernel(ids, pattern, near, far, plan, pat, need):
    agg, col = ids[0], ids[1]
    base = (agg - 2) * 4
    for k in range(16):
        pat[k] = far[k]
        pat[16 + k] = near[k]
        pat[32 + k] = pattern[k // 4, k % 4]
    for k in range(32):
        need[k] = 0

    def through(row, index, target, m):
        inner = pat[4 * row + m]
        at = jnp.clip(inner - base, 0, ROWS - 1)
        n = jnp.int32(0)
        for q in range(1, 4):
            n = jnp.where(pat[4 * at + q] == target, q, n)
        valid = (inner < jnp.minimum(index, target)) & (n > 0)
        return at, n, valid

    count = jnp.int32(0)
    for r in range(4):
        row = 8 + r
        index = base + row
        target = pat[4 * row + col]
        lower = target < index
        diagonal = jnp.where(lower, jnp.clip(target - base, 4, ROWS - 1), row) - 4
        need[col * 8 + row - 4] = 1
        need[diagonal] = 1
        for m in range(1, 4):
            at, n, valid = through(row, index, target, m)
            x, y = m * 8 + row - 4, n * 8 + jnp.maximum(at - 4, 0)
            plan[LIST2 + count] = x | (y << 8) | (r << 16)
            count = count + valid.astype(jnp.int32)

            @pl.when(valid)
            def _():
                need[x] = 1
                need[y] = 1

        own = col * 8 + row - 4
        x = jnp.where(lower, own, 40 + row - 4)
        y = jnp.where(target > index, own, 32 + diagonal)
        plan[LIST2 + count] = x | (y << 8) | (r << 16)
        count = count + 1
        kind = jnp.where(lower, 1, jnp.where(target == index, 2, 0))
        plan[KINDS + r] = kind | (diagonal << 8)
    plan[1] = count

    def tile(t, carry):
        @pl.when(need[t] == 1)
        def _():
            products, tiles = plan[0], plan[2]
            row = (t & 7) + 4
            slot = t >> 3
            index = base + row
            target = pat[4 * row + slot]
            lower = target < index
            diagonal = jnp.where(lower, jnp.clip(target - base, 4, ROWS - 1), row) - 4
            for m in range(1, 4):
                at, n, valid = through(row, index, target, m)
                plan[LIST1 + products] = (m * ROWS + row) | ((n * ROWS + at) << 8) | (t << 16)
                products = products + valid.astype(jnp.int32)
            own = slot * ROWS + row
            x = jnp.where(lower, own, 56 + row - 4)
            y = jnp.where(target > index, own, 48 + diagonal)
            plan[LIST1 + products] = x | (y << 8) | (t << 16)
            plan[0] = products + 1
            kind = jnp.where(lower, 1, jnp.where(target == index, 2, 0))
            plan[TILES + tiles] = t | (kind << 8) | (diagonal << 16)
            plan[2] = tiles + 1

        return carry

    plan[0] = 0
    plan[2] = 0
    lax.fori_loop(0, 32, tile, 0)
    for u in range(STEP - 1):
        plan[LIST1 + plan[0] + u] = ZERO1 | (ZERO1 << 8) | (32 << 16)


def sweep_kernel(ids, plan, coarse, *refs):
    pieces, (out, arrived, first, work, high, low, pivots, pivots_next, sems) = refs[:12], refs[12:]
    col = ids[1]
    width = coarse.shape[-1]
    copies = []
    for k, piece in enumerate(pieces):
        copies.append(pltpu.make_async_copy(piece, arrived.at[pl.ds(4 * k, 4)], sems.at[k]))
        copies[-1].start()
    first[ZERO1] = jnp.zeros((width, width), BF16)
    lines, columns = iota((width, width), 0), iota((width, width), 1)
    upper, lower, equal = columns > lines, lines > columns, lines == columns

    def reciprocal(tile):
        return 1.0 / jnp.maximum(jnp.sum(jnp.where(equal, tile, 0.0), axis=0, keepdims=True), 1.0)

    for k, copy in enumerate(copies):
        copy.wait()
        start = ((col + (0, 3, 1, 2)[k % 4]) & 3) * ROWS + k // 4 * 4
        for r in range(4):
            store_unpacked(first.at[start + r], arrived[4 * k + r], width)

    def prepare(k, carry):
        diagonal = first[4 + k].astype(F32)
        first[48 + k] = jnp.where(upper, diagonal, 0.0).astype(BF16)
        first[56 + k] = jnp.where(lower, diagonal, 0.0).astype(BF16)
        pivots[k] = reciprocal(diagonal)
        return carry

    lax.fori_loop(0, 8, prepare, 0)

    def begin(k, carry):
        t = plan[TILES + k] & 255
        work[t] = first[(t >> 3) * ROWS + (t & 7) + 4].astype(F32)
        return carry

    lax.fori_loop(0, plan[2], begin, 0)

    def multiply(k, carry):
        entries = entries_of(plan, LIST1, k)
        products = [jnp.dot(first[e & 255], first[(e >> 8) & 255], preferred_element_type=F32) for e in entries]
        for e, product in zip(entries, products):
            work[e >> 16] -= product
        return carry

    lax.fori_loop(0, (plan[0] + STEP - 1) // STEP, multiply, 0)

    def scaled(tile, kind, row):
        factor = jnp.where((kind == 1) | ((kind == 2) & lower), row, 1.0)
        return tile * factor

    def split(t, tile):
        top = tile.astype(BF16)
        high[t] = top
        low[t] = (tile - top.astype(F32)).astype(BF16)

    def finish(k, carry):
        entry = plan[TILES + k]
        t, kind, diagonal = entry & 255, (entry >> 8) & 255, entry >> 16
        tile = scaled(work[t], kind, pivots[diagonal])
        split(t, tile)

        @pl.when(t < 8)
        def _():
            split(32 + t, jnp.where(upper, tile, 0.0))
            split(40 + t, jnp.where(lower, tile, 0.0))
            pivots_next[t] = reciprocal(tile)

        return carry

    lax.fori_loop(0, plan[2], finish, 0)
    out[...] = coarse[...]

    def again(k, carry):
        entry = plan[LIST2 + k]
        x, y, r = entry & 255, (entry >> 8) & 255, entry >> 16
        product = jnp.dot(high[x], high[y], preferred_element_type=F32)
        product += jnp.dot(high[x], low[y], preferred_element_type=F32)
        product += jnp.dot(low[x], high[y], preferred_element_type=F32)
        out[r] -= product
        return carry

    lax.fori_loop(0, plan[1], again, 0)
    for r in range(4):
        entry = plan[KINDS + r]
        out[r] = scaled(out[r], entry & 255, pivots_next[entry >> 8])


def along(block, axis, distance, ring=False, sources=None):
    count = lax.axis_size(axis)
    pairs = [(i, (i + distance) % count) for i in range(count) if ring or 0 <= i + distance < count]
    return lax.ppermute(block, axis, [pair for pair in pairs if sources is None or pair[0] in sources])


def on_device(fine_tiles, fine_cols, agg_of, prolong, coarse_cols):
    rows, width = prolong.shape[0], prolong.shape[-1]
    agg, col = lax.axis_index("agg"), lax.axis_index("col")
    ids = jnp.stack([agg, col]).astype(jnp.int32)
    packed = packed_shape(width)
    four, four_packed = (4, width, width), (4, *packed)

    def array(shape, dtype):
        return jax.ShapeDtypeStruct(shape, dtype)

    def call(kernel, ins, outs, out_specs, scratch, name, mebibytes):
        return pl.pallas_call(
            kernel,
            out_shape=outs,
            in_specs=ins,
            out_specs=out_specs,
            scratch_shapes=scratch,
            name=name,
            compiler_params=pltpu.CompilerParams(vmem_limit_bytes=mebibytes << 20),
        )

    cols = fine_cols.reshape(-1)
    tiles = fine_tiles.reshape(rows, width, width)
    halo_shape = (rows * packed[0] + 16, 128)
    halo = call(pack_kernel, [SMEM] * 2 + [VMEM], array(halo_shape, BF16), VMEM, [], "pack", 60)(
        agg_of, coarse_cols, prolong
    )
    left, right = along(halo, "agg", 1), along(halo, "agg", -1)
    total, turned = call(
        close_kernel,
        [SMEM] * 4 + [VMEM] * 2,
        (array((SPARE + 1, width, width), F32), array((rows, width, width), BF16)),
        (VMEM, VMEM),
        [pltpu.SMEM((20,), jnp.int32)],
        "close",
        14,
    )(ids, cols, agg_of, coarse_cols, tiles, prolong)
    mine, ahead, behind, near = call(
        distant_kernel,
        [SMEM] * 4 + [VMEM] * 5,
        (array(four, F32), array(four_packed, BF16), array(four_packed, BF16), array((16,), jnp.int32)),
        (VMEM, VMEM, VMEM, SMEM),
        [
            pltpu.VMEM((SPARE + 1, width, width), F32),
            pltpu.VMEM((STEP, width, width), BF16),
            pltpu.VMEM((32, 128), jnp.int32),
            pltpu.SMEM((32, 128), jnp.int32),
            pltpu.SMEM((20,), jnp.int32),
            pltpu.SemaphoreType.DMA,
        ],
        "distant",
        22,
    )(ids, cols, agg_of, coarse_cols, tiles, turned, left, right, total)

    came_ahead = lax.ppermute(ahead, "col", [(1, 2), (2, 3), (3, 1)])
    came_behind = lax.ppermute(behind, "col", [(1, 3), (2, 1), (3, 2)])
    far = along(near, "agg", 1)
    plan = call(
        plan_kernel,
        [SMEM] * 4,
        array((PLAN,), jnp.int32),
        SMEM,
        [pltpu.SMEM((48,), jnp.int32), pltpu.SMEM((32,), jnp.int32)],
        "plan",
        4,
    )(ids, coarse_cols, near, far)
    coarse, sent, kept = call(
        combine_kernel,
        [SMEM] + [VMEM] * 3,
        (array(four, F32), array(four_packed, BF16), array(four, F32)),
        (VMEM, VMEM, VMEM),
        [pltpu.VMEM((width, width), F32)],
        "combine",
        8,
    )(plan, mine, came_ahead, came_behind)

    here = [sent] + [along(sent, "col", d, True) for d in (1, -1, 2)]
    before = [along(x, "agg", 1) for x in here]
    others = (1, 2, 3)
    second = along(sent, "agg", 2)
    further = [second] + [along(second, "col", d, True, others) for d in (1, -1)] + [along(before[3], "agg", 1)]
    factor = call(
        sweep_kernel,
        [SMEM] * 2 + [VMEM] + [ANY] * 12,
        array(four, F32),
        VMEM,
        [
            pltpu.VMEM((48, *packed), BF16),
            pltpu.VMEM((65, width, width), BF16),
            pltpu.VMEM((33, width, width), F32),
            pltpu.VMEM((49, width, width), BF16),
            pltpu.VMEM((49, width, width), BF16),
            pltpu.VMEM((8, 1, width), F32),
            pltpu.VMEM((8, 1, width), F32),
            pltpu.SemaphoreType.DMA((12,)),
        ],
        "sweep",
        34,
    )(ids, plan, kept, *further, *before, *here)
    return (coarse[:, None], factor[:, None])


def solution(mesh):
    in_specs = (
        P("agg", "col", None, None),
        P("agg", "col"),
        P("agg"),
        P("agg", None, None),
        P("agg", None),
    )
    out_specs = (P("agg", "col", None, None), P("agg", "col", None, None))
    return jax.shard_map(
        on_device, mesh=mesh, in_specs=in_specs, out_specs=out_specs, check_vma=False
    )
```

```python
import functools

import jax
import jax.numpy as jnp
from jax import lax
from jax.experimental import pallas as pl
from jax.experimental.pallas import tpu as pltpu
from jax.sharding import PartitionSpec as P

F32 = jnp.float32
BF16 = jnp.bfloat16
VMEM = pl.BlockSpec(memory_space=pltpu.VMEM)
SMEM = pl.BlockSpec(memory_space=pltpu.SMEM)
ANY = pl.BlockSpec(memory_space=pl.ANY)

ROWS = 12
LIST1 = 16
LIST2 = 160
TILES = 192
KINDS = 240
PLAN = 256
STEP = 4
ZERO1 = 64
SPARE = 16


def iota(shape, dim):
    return lax.broadcasted_iota(jnp.int32, shape, dim)


def packed_shape(width):
    return (width * width // 128, 128)


def store_packed(ref, tile):
    width, half = tile.shape[0], tile.shape[0] // 2
    ref[:width] = tile[:, :128]
    ref[width:] = jnp.concatenate([tile[:half, 128:], tile[half:, 128:]], axis=1)


def store_unpacked(ref, packed, width):
    half, rest = width // 2, width - 128
    ref[:, :128] = packed[:width]
    ref[:half, 128:] = packed[width:, :rest]
    ref[half:, 128:] = packed[width:, rest:]


def pack_kernel(labels, pattern, source, packed, tiles, sems):
    copies = []
    for k in range(4):
        part = pl.ds(4 * k, 4)
        copies.append(pltpu.make_async_copy(source.at[part], tiles.at[part], sems.at[k]))
        copies[-1].start()
    count, size = tiles.shape[0], tiles.shape[1] * tiles.shape[2] // 128
    line, lane = iota((16, 128), 0), iota((16, 128), 1)
    about = jnp.zeros((16, 128), F32)
    for i in range(count):
        about = jnp.where((line == 0) & (lane == i), (labels[i] & 3).astype(F32), about)
    for r in range(4):
        for q in range(1, 4):
            offset = pattern[r, q] - pattern[r, 0]
            about = jnp.where((line == 1) & (lane == 4 * r + q), offset.astype(F32), about)
    packed[count * size :] = about.astype(BF16)
    for i in range(count):
        if i % 4 == 0:
            copies[i // 4].wait()
        store_packed(packed.at[pl.ds(i * size, size)], tiles[i])


def entries_of(plan, start, k):
    return [plan[start + STEP * k + u] for u in range(STEP)]


def add_lifted(entries, tiles, turned, remote, total):
    carried = [
        jnp.dot(tiles[e & 255], remote(u, (e >> 8) & 255), preferred_element_type=F32).astype(BF16)
        for u, e in enumerate(entries)
    ]
    lifted = [
        jnp.dot(turned[e & 255], c, preferred_element_type=F32) for e, c in zip(entries, carried)
    ]
    for e, tile in zip(entries, lifted):
        total[e >> 16] += tile


def slot_of(pattern, row, target):
    slot = jnp.int32(0)
    for q in range(1, 4):
        slot = jnp.where(pattern[row, q] == target, q, slot)
    return slot


def close_kernel(ids, cols, labels, pattern, tiles, own, total, turned, work):
    agg = ids[0]

    def note(i, count):
        place = cols[i] - agg * 16
        row = labels[i] & 3
        slot = slot_of(pattern, row, labels[place & 15])
        work[count] = i | ((place & 15) << 8) | ((slot * 4 + row) << 16)
        return count + (place >> 4 == 0).astype(jnp.int32)

    count = lax.fori_loop(0, 16, note, jnp.int32(0))
    for u in range(STEP - 1):
        work[count + u] = SPARE << 16
    total[...] = jnp.zeros_like(total)

    def turn(i, carry):
        turned[i] = own[i].T
        return carry

    lax.fori_loop(0, 16, turn, 0)

    def step(k, carry):
        add_lifted(entries_of(work, 0, k), tiles, turned, lambda u, place: own[place], total)
        return carry

    lax.fori_loop(0, (count + STEP - 1) // STEP, step, 0)


def distant_kernel(ids, cols, labels, pattern, tiles, turned, left, right, begun, *refs):
    mine, ahead, behind, near, total, remote, seen, about, work, sem = refs
    agg, col = ids[0], ids[1]
    width = tiles.shape[-1]
    size = width * width // 128
    end = 16 * size
    seen[:16] = left[end:].astype(F32).astype(jnp.int32)
    seen[16:] = right[end:].astype(F32).astype(jnp.int32)
    copy = pltpu.make_async_copy(seen, about, sem)
    copy.start()
    total[...] = begun[...]
    copy.wait()

    def note(i, count):
        place = cols[i] - (agg - 1) * 16
        side, within = place >> 4, place & 15
        target = jnp.where(side == 0, about[0, within] + 4 * agg - 4, about[16, within] + 4 * agg + 4)
        row = labels[i] & 3
        slot = slot_of(pattern, row, target)
        work[count] = i | ((within + jnp.where(side == 0, 0, 16)) << 8) | ((slot * 4 + row) << 16)
        return count + (side != 1).astype(jnp.int32)

    count = lax.fori_loop(0, 16, note, jnp.int32(0))
    for u in range(STEP - 1):
        work[count + u] = SPARE << 16
    for k in range(16):
        near[k] = 4 * agg - 4 + k // 4 + about[1, k]

    def step(k, carry):
        entries = entries_of(work, 0, k)
        for u, e in enumerate(entries):
            place = (e >> 8) & 255
            start = pl.multiple_of((place & 15) * size, 16)

            @pl.when(place < 16)
            def _():
                store_unpacked(remote.at[u], left[pl.ds(start, size)], width)

            @pl.when(place >= 16)
            def _():
                store_unpacked(remote.at[u], right[pl.ds(start, size)], width)

        add_lifted(entries, tiles, turned, lambda u, place: remote[u], total)
        return carry

    lax.fori_loop(0, (count + STEP - 1) // STEP, step, 0)
    first = jnp.where(col == 3, 1, col + 1)
    second = jnp.where(col <= 1, 3, col - 1)
    for r in range(4):
        mine[r] = total[col * 4 + r]
        store_packed(ahead.at[r], total[first * 4 + r].astype(BF16))
        store_packed(behind.at[r], total[second * 4 + r].astype(BF16))


def combine_kernel(plan, mine, ahead, behind, coarse, sent, kept, wide):
    width = mine.shape[-1]
    for r in range(4):
        store_unpacked(wide, ahead[r].astype(F32) + behind[r].astype(F32), width)
        tile = mine[r] + wide[...]
        coarse[r] = tile
        kept[r] = tile
        store_packed(sent.at[r], tile.astype(BF16))


def plan_kernel(ids, pattern, near, far, plan, pat, need):
    agg, col = ids[0], ids[1]
    base = (agg - 2) * 4
    for k in range(16):
        pat[k] = far[k]
        pat[16 + k] = near[k]
        pat[32 + k] = pattern[k // 4, k % 4]
    for k in range(32):
        need[k] = 0

    def through(row, index, target, m):
        inner = pat[4 * row + m]
        at = jnp.clip(inner - base, 0, ROWS - 1)
        n = jnp.int32(0)
        for q in range(1, 4):
            n = jnp.where(pat[4 * at + q] == target, q, n)
        valid = (inner < jnp.minimum(index, target)) & (n > 0)
        return at, n, valid

    count = jnp.int32(0)
    for r in range(4):
        row = 8 + r
        index = base + row
        target = pat[4 * row + col]
        lower = target < index
        diagonal = jnp.where(lower, jnp.clip(target - base, 4, ROWS - 1), row) - 4
        need[col * 8 + row - 4] = 1
        need[diagonal] = 1
        for m in range(1, 4):
            at, n, valid = through(row, index, target, m)
            x, y = m * 8 + row - 4, n * 8 + jnp.maximum(at - 4, 0)
            plan[LIST2 + count] = x | (y << 8) | (r << 16)
            count = count + valid.astype(jnp.int32)

            @pl.when(valid)
            def _():
                need[x] = 1
                need[y] = 1

        own = col * 8 + row - 4
        x = jnp.where(lower, own, 40 + row - 4)
        y = jnp.where(target > index, own, 32 + diagonal)
        plan[LIST2 + count] = x | (y << 8) | (r << 16)
        count = count + 1
        kind = jnp.where(lower, 1, jnp.where(target == index, 2, 0))
        plan[KINDS + r] = kind | (diagonal << 8)
    plan[1] = count

    def tile(t, carry):
        @pl.when(need[t] == 1)
        def _():
            products, tiles = plan[0], plan[2]
            row = (t & 7) + 4
            slot = t >> 3
            index = base + row
            target = pat[4 * row + slot]
            lower = target < index
            diagonal = jnp.where(lower, jnp.clip(target - base, 4, ROWS - 1), row) - 4
            for m in range(1, 4):
                at, n, valid = through(row, index, target, m)
                plan[LIST1 + products] = (m * ROWS + row) | ((n * ROWS + at) << 8) | (t << 16)
                products = products + valid.astype(jnp.int32)
            own = slot * ROWS + row
            x = jnp.where(lower, own, 56 + row - 4)
            y = jnp.where(target > index, own, 48 + diagonal)
            plan[LIST1 + products] = x | (y << 8) | (t << 16)
            plan[0] = products + 1
            kind = jnp.where(lower, 1, jnp.where(target == index, 2, 0))
            plan[TILES + tiles] = t | (kind << 8) | (diagonal << 16)
            plan[2] = tiles + 1

        return carry

    plan[0] = 0
    plan[2] = 0
    lax.fori_loop(0, 32, tile, 0)
    for u in range(STEP - 1):
        plan[LIST1 + plan[0] + u] = ZERO1 | (ZERO1 << 8) | (32 << 16)


def sweep_kernel(ids, plan, coarse, *refs):
    pieces, (out, first, work, high, low, pivots, pivots_next) = refs[:12], refs[12:]
    col = ids[1]
    width = coarse.shape[-1]
    first[ZERO1] = jnp.zeros((width, width), BF16)
    lines, columns = iota((width, width), 0), iota((width, width), 1)
    upper, lower, equal = columns > lines, lines > columns, lines == columns

    def reciprocal(tile):
        return 1.0 / jnp.maximum(jnp.sum(jnp.where(equal, tile, 0.0), axis=0, keepdims=True), 1.0)

    for k, piece in enumerate(pieces):
        start = ((col + (0, 3, 1, 2)[k % 4]) & 3) * ROWS + k // 4 * 4
        for r in range(4):
            store_unpacked(first.at[start + r], piece[r], width)

    def prepare(k, carry):
        diagonal = first[4 + k].astype(F32)
        first[48 + k] = jnp.where(upper, diagonal, 0.0).astype(BF16)
        first[56 + k] = jnp.where(lower, diagonal, 0.0).astype(BF16)
        pivots[k] = reciprocal(diagonal)
        return carry

    lax.fori_loop(0, 8, prepare, 0)

    def begin(k, carry):
        t = plan[TILES + k] & 255
        work[t] = first[(t >> 3) * ROWS + (t & 7) + 4].astype(F32)
        return carry

    lax.fori_loop(0, plan[2], begin, 0)

    def multiply(k, carry):
        entries = entries_of(plan, LIST1, k)
        products = [jnp.dot(first[e & 255], first[(e >> 8) & 255], preferred_element_type=F32) for e in entries]
        for e, product in zip(entries, products):
            work[e >> 16] -= product
        return carry

    lax.fori_loop(0, (plan[0] + STEP - 1) // STEP, multiply, 0)

    def scaled(tile, kind, row):
        factor = jnp.where((kind == 1) | ((kind == 2) & lower), row, 1.0)
        return tile * factor

    def split(t, tile):
        top = tile.astype(BF16)
        high[t] = top
        low[t] = (tile - top.astype(F32)).astype(BF16)

    def finish(k, carry):
        entry = plan[TILES + k]
        t, kind, diagonal = entry & 255, (entry >> 8) & 255, entry >> 16
        tile = scaled(work[t], kind, pivots[diagonal])
        split(t, tile)

        @pl.when(t < 8)
        def _():
            split(32 + t, jnp.where(upper, tile, 0.0))
            split(40 + t, jnp.where(lower, tile, 0.0))
            pivots_next[t] = reciprocal(tile)

        return carry

    lax.fori_loop(0, plan[2], finish, 0)
    out[...] = coarse[...]

    def again(k, carry):
        entry = plan[LIST2 + k]
        x, y, r = entry & 255, (entry >> 8) & 255, entry >> 16
        product = jnp.dot(high[x], high[y], preferred_element_type=F32)
        product += jnp.dot(high[x], low[y], preferred_element_type=F32)
        product += jnp.dot(low[x], high[y], preferred_element_type=F32)
        out[r] -= product
        return carry

    lax.fori_loop(0, plan[1], again, 0)
    for r in range(4):
        entry = plan[KINDS + r]
        out[r] = scaled(out[r], entry & 255, pivots_next[entry >> 8])


def along(block, axis, distance, ring=False, sources=None):
    count = lax.axis_size(axis)
    pairs = [(i, (i + distance) % count) for i in range(count) if ring or 0 <= i + distance < count]
    return lax.ppermute(block, axis, [pair for pair in pairs if sources is None or pair[0] in sources])


def on_device(fine_tiles, fine_cols, agg_of, prolong, coarse_cols):
    rows, width = prolong.shape[0], prolong.shape[-1]
    agg, col = lax.axis_index("agg"), lax.axis_index("col")
    ids = jnp.stack([agg, col]).astype(jnp.int32)
    packed = packed_shape(width)
    four, four_packed = (4, width, width), (4, *packed)

    def array(shape, dtype):
        return jax.ShapeDtypeStruct(shape, dtype)

    def call(kernel, ins, outs, out_specs, scratch, name, mebibytes):
        return pl.pallas_call(
            kernel,
            out_shape=outs,
            in_specs=ins,
            out_specs=out_specs,
            scratch_shapes=scratch,
            name=name,
            compiler_params=pltpu.CompilerParams(vmem_limit_bytes=mebibytes << 20),
        )

    cols = fine_cols.reshape(-1)
    tiles = fine_tiles.reshape(rows, width, width)
    halo_shape = (rows * packed[0] + 16, 128)
    halo = call(
        pack_kernel,
        [SMEM] * 2 + [ANY],
        array(halo_shape, BF16),
        VMEM,
        [pltpu.VMEM((rows, width, width), BF16), pltpu.SemaphoreType.DMA((4,))],
        "pack",
        60,
    )(agg_of, coarse_cols, prolong)
    left, right = along(halo, "agg", 1), along(halo, "agg", -1)
    total, turned = call(
        close_kernel,
        [SMEM] * 4 + [VMEM] * 2,
        (array((SPARE + 1, width, width), F32), array((rows, width, width), BF16)),
        (VMEM, VMEM),
        [pltpu.SMEM((20,), jnp.int32)],
        "close",
        14,
    )(ids, cols, agg_of, coarse_cols, tiles, prolong)
    mine, ahead, behind, near = call(
        distant_kernel,
        [SMEM] * 4 + [VMEM] * 5,
        (array(four, F32), array(four_packed, BF16), array(four_packed, BF16), array((16,), jnp.int32)),
        (VMEM, VMEM, VMEM, SMEM),
        [
            pltpu.VMEM((SPARE + 1, width, width), F32),
            pltpu.VMEM((STEP, width, width), BF16),
            pltpu.VMEM((32, 128), jnp.int32),
            pltpu.SMEM((32, 128), jnp.int32),
            pltpu.SMEM((20,), jnp.int32),
            pltpu.SemaphoreType.DMA,
        ],
        "distant",
        22,
    )(ids, cols, agg_of, coarse_cols, tiles, turned, left, right, total)

    came_ahead = lax.ppermute(ahead, "col", [(1, 2), (2, 3), (3, 1)])
    came_behind = lax.ppermute(behind, "col", [(1, 3), (2, 1), (3, 2)])
    far = along(near, "agg", 1)
    plan = call(
        plan_kernel,
        [SMEM] * 4,
        array((PLAN,), jnp.int32),
        SMEM,
        [pltpu.SMEM((48,), jnp.int32), pltpu.SMEM((32,), jnp.int32)],
        "plan",
        4,
    )(ids, coarse_cols, near, far)
    coarse, sent, kept = call(
        combine_kernel,
        [SMEM] + [VMEM] * 3,
        (array(four, F32), array(four_packed, BF16), array(four, F32)),
        (VMEM, VMEM, VMEM),
        [pltpu.VMEM((width, width), F32)],
        "combine",
        8,
    )(plan, mine, came_ahead, came_behind)

    here = [sent] + [along(sent, "col", d, True) for d in (1, -1, 2)]
    before = [along(x, "agg", 1) for x in here]
    others = (1, 2, 3)
    second = along(sent, "agg", 2)
    further = [second] + [along(second, "col", d, True, others) for d in (1, -1)] + [along(before[3], "agg", 1)]
    factor = call(
        sweep_kernel,
        [SMEM] * 2 + [VMEM] * 13,
        array(four, F32),
        VMEM,
        [
            pltpu.VMEM((65, width, width), BF16),
            pltpu.VMEM((33, width, width), F32),
            pltpu.VMEM((49, width, width), BF16),
            pltpu.VMEM((49, width, width), BF16),
            pltpu.VMEM((8, 1, width), F32),
            pltpu.VMEM((8, 1, width), F32),
        ],
        "sweep",
        34,
    )(ids, plan, kept, *further, *before, *here)
    return (coarse[:, None], factor[:, None])


def solution(mesh):
    in_specs = (
        P("agg", "col", None, None),
        P("agg", "col"),
        P("agg"),
        P("agg", None, None),
        P("agg", None),
    )
    out_specs = (P("agg", "col", None, None), P("agg", "col", None, None))
    return jax.shard_map(
        on_device, mesh=mesh, in_specs=in_specs, out_specs=out_specs, check_vma=False
    )
```

```python
import functools

import jax
import jax.numpy as jnp
from jax import lax
from jax.experimental import pallas as pl
from jax.experimental.pallas import tpu as pltpu
from jax.sharding import PartitionSpec as P

F32 = jnp.float32
BF16 = jnp.bfloat16
VMEM = pl.BlockSpec(memory_space=pltpu.VMEM)
SMEM = pl.BlockSpec(memory_space=pltpu.SMEM)
ANY = pl.BlockSpec(memory_space=pl.ANY)

ROWS = 12
LIST1 = 16
LIST2 = 160
TILES = 192
KINDS = 240
PLAN = 256
STEP = 4
ZERO1 = 64
ZERO2 = 48
SPARE = 16


def iota(shape, dim):
    return lax.broadcasted_iota(jnp.int32, shape, dim)


def packed_shape(width):
    return (width * width // 128, 128)


def store_packed(ref, tile):
    width, half = tile.shape[0], tile.shape[0] // 2
    ref[:width] = tile[:, :128]
    ref[width:] = jnp.concatenate([tile[:half, 128:], tile[half:, 128:]], axis=1)


def store_unpacked(ref, packed, width):
    half, rest = width // 2, width - 128
    ref[:, :128] = packed[:width]
    ref[:half, 128:] = packed[width:, :rest]
    ref[half:, 128:] = packed[width:, rest:]


def pack_kernel(labels, pattern, tiles, packed):
    count, size = tiles.shape[0], tiles.shape[1] * tiles.shape[2] // 128
    line, lane = iota((16, 128), 0), iota((16, 128), 1)
    about = jnp.zeros((16, 128), F32)
    for i in range(count):
        about = jnp.where((line == 0) & (lane == i), (labels[i] & 3).astype(F32), about)
    for r in range(4):
        for q in range(1, 4):
            offset = pattern[r, q] - pattern[r, 0]
            about = jnp.where((line == 1) & (lane == 4 * r + q), offset.astype(F32), about)
    packed[count * size :] = about.astype(BF16)
    for i in range(count):
        store_packed(packed.at[pl.ds(i * size, size)], tiles[i])


def entries_of(plan, start, k):
    return [plan[start + STEP * k + u] for u in range(STEP)]


def add_lifted(entries, tiles, turned, remote, total):
    carried = [
        jnp.dot(tiles[e & 255], remote(u, (e >> 8) & 255), preferred_element_type=F32).astype(BF16)
        for u, e in enumerate(entries)
    ]
    lifted = [
        jnp.dot(turned[e & 255], c, preferred_element_type=F32) for e, c in zip(entries, carried)
    ]
    for e, tile in zip(entries, lifted):
        total[e >> 16] += tile


def slot_of(pattern, row, target):
    slot = jnp.int32(0)
    for q in range(1, 4):
        slot = jnp.where(pattern[row, q] == target, q, slot)
    return slot


def close_kernel(ids, cols, labels, pattern, tiles, own, total, turned, work):
    agg = ids[0]

    def note(i, count):
        place = cols[i] - agg * 16
        row = labels[i] & 3
        slot = slot_of(pattern, row, labels[place & 15])
        work[count] = i | ((place & 15) << 8) | ((slot * 4 + row) << 16)
        return count + (place >> 4 == 0).astype(jnp.int32)

    count = lax.fori_loop(0, 16, note, jnp.int32(0))
    for u in range(STEP - 1):
        work[count + u] = SPARE << 16
    total[...] = jnp.zeros_like(total)

    def turn(i, carry):
        turned[i] = own[i].T
        return carry

    lax.fori_loop(0, 16, turn, 0)

    def step(k, carry):
        add_lifted(entries_of(work, 0, k), tiles, turned, lambda u, place: own[place], total)
        return carry

    lax.fori_loop(0, (count + STEP - 1) // STEP, step, 0)


def distant_kernel(ids, cols, labels, pattern, tiles, turned, left, right, begun, *refs):
    mine, ahead, behind, near, total, remote, seen, about, work, sem = refs
    agg, col = ids[0], ids[1]
    width = tiles.shape[-1]
    size = width * width // 128
    end = 16 * size
    seen[:16] = left[end:].astype(F32).astype(jnp.int32)
    seen[16:] = right[end:].astype(F32).astype(jnp.int32)
    copy = pltpu.make_async_copy(seen, about, sem)
    copy.start()
    total[...] = begun[...]
    copy.wait()

    def note(i, count):
        place = cols[i] - (agg - 1) * 16
        side, within = place >> 4, place & 15
        target = jnp.where(side == 0, about[0, within] + 4 * agg - 4, about[16, within] + 4 * agg + 4)
        row = labels[i] & 3
        slot = slot_of(pattern, row, target)
        work[count] = i | ((within + jnp.where(side == 0, 0, 16)) << 8) | ((slot * 4 + row) << 16)
        return count + (side != 1).astype(jnp.int32)

    count = lax.fori_loop(0, 16, note, jnp.int32(0))
    for u in range(STEP - 1):
        work[count + u] = SPARE << 16
    for k in range(16):
        near[k] = 4 * agg - 4 + k // 4 + about[1, k]

    def step(k, carry):
        entries = entries_of(work, 0, k)
        for u, e in enumerate(entries):
            place = (e >> 8) & 255
            start = pl.multiple_of((place & 15) * size, 16)

            @pl.when(place < 16)
            def _():
                store_unpacked(remote.at[u], left[pl.ds(start, size)], width)

            @pl.when(place >= 16)
            def _():
                store_unpacked(remote.at[u], right[pl.ds(start, size)], width)

        add_lifted(entries, tiles, turned, lambda u, place: remote[u], total)
        return carry

    lax.fori_loop(0, (count + STEP - 1) // STEP, step, 0)
    first = jnp.where(col == 3, 1, col + 1)
    second = jnp.where(col <= 1, 3, col - 1)
    for r in range(4):
        mine[r] = total[col * 4 + r]
        store_packed(ahead.at[r], total[first * 4 + r].astype(BF16))
        store_packed(behind.at[r], total[second * 4 + r].astype(BF16))


def combine_kernel(plan, mine, ahead, behind, coarse, sent, kept, wide):
    width = mine.shape[-1]
    for r in range(4):
        store_unpacked(wide, ahead[r].astype(F32) + behind[r].astype(F32), width)
        tile = mine[r] + wide[...]
        coarse[r] = tile
        kept[r] = tile
        store_packed(sent.at[r], tile.astype(BF16))


def plan_kernel(ids, pattern, near, far, plan, pat, need):
    agg, col = ids[0], ids[1]
    base = (agg - 2) * 4
    for k in range(16):
        pat[k] = far[k]
        pat[16 + k] = near[k]
        pat[32 + k] = pattern[k // 4, k % 4]
    for k in range(32):
        need[k] = 0

    def through(row, index, target, m):
        inner = pat[4 * row + m]
        at = jnp.clip(inner - base, 0, ROWS - 1)
        n = jnp.int32(0)
        for q in range(1, 4):
            n = jnp.where(pat[4 * at + q] == target, q, n)
        valid = (inner < jnp.minimum(index, target)) & (n > 0)
        return at, n, valid

    count = jnp.int32(0)
    for r in range(4):
        row = 8 + r
        index = base + row
        target = pat[4 * row + col]
        lower = target < index
        diagonal = jnp.where(lower, jnp.clip(target - base, 4, ROWS - 1), row) - 4
        need[col * 8 + row - 4] = 1
        need[diagonal] = 1
        for m in range(1, 4):
            at, n, valid = through(row, index, target, m)
            x, y = m * 8 + row - 4, n * 8 + jnp.maximum(at - 4, 0)
            plan[LIST2 + count] = x | (y << 8) | (r << 16)
            count = count + valid.astype(jnp.int32)

            @pl.when(valid)
            def _():
                need[x] = 1
                need[y] = 1

        own = col * 8 + row - 4
        x = jnp.where(lower, own, 40 + row - 4)
        y = jnp.where(target > index, own, 32 + diagonal)
        plan[LIST2 + count] = x | (y << 8) | (r << 16)
        count = count + 1
        kind = jnp.where(lower, 1, jnp.where(target == index, 2, 0))
        plan[KINDS + r] = kind | (diagonal << 8)
    plan[1] = count
    for u in range(STEP - 1):
        plan[LIST2 + count + u] = ZERO2 | (ZERO2 << 8)

    def tile(t, carry):
        @pl.when(need[t] == 1)
        def _():
            products, tiles = plan[0], plan[2]
            row = (t & 7) + 4
            slot = t >> 3
            index = base + row
            target = pat[4 * row + slot]
            lower = target < index
            diagonal = jnp.where(lower, jnp.clip(target - base, 4, ROWS - 1), row) - 4
            for m in range(1, 4):
                at, n, valid = through(row, index, target, m)
                plan[LIST1 + products] = (m * ROWS + row) | ((n * ROWS + at) << 8) | (t << 16)
                products = products + valid.astype(jnp.int32)
            own = slot * ROWS + row
            x = jnp.where(lower, own, 56 + row - 4)
            y = jnp.where(target > index, own, 48 + diagonal)
            plan[LIST1 + products] = x | (y << 8) | (t << 16)
            plan[0] = products + 1
            kind = jnp.where(lower, 1, jnp.where(target == index, 2, 0))
            plan[TILES + tiles] = t | (kind << 8) | (diagonal << 16)
            plan[2] = tiles + 1

        return carry

    plan[0] = 0
    plan[2] = 0
    lax.fori_loop(0, 32, tile, 0)
    for u in range(STEP - 1):
        plan[LIST1 + plan[0] + u] = ZERO1 | (ZERO1 << 8) | (32 << 16)


def sweep_kernel(ids, plan, coarse, *refs):
    pieces, (out, first, work, high, low, pivots, pivots_next) = refs[:12], refs[12:]
    col = ids[1]
    width = coarse.shape[-1]
    first[ZERO1] = jnp.zeros((width, width), BF16)
    high[ZERO2] = jnp.zeros((width, width), BF16)
    low[ZERO2] = jnp.zeros((width, width), BF16)
    lines, columns = iota((width, width), 0), iota((width, width), 1)
    upper, lower, equal = columns > lines, lines > columns, lines == columns

    def reciprocal(tile):
        return 1.0 / jnp.maximum(jnp.sum(jnp.where(equal, tile, 0.0), axis=0, keepdims=True), 1.0)

    for k, piece in enumerate(pieces):
        start = ((col + (0, 3, 1, 2)[k % 4]) & 3) * ROWS + k // 4 * 4
        for r in range(4):
            store_unpacked(first.at[start + r], piece[r], width)

    def prepare(k, carry):
        diagonal = first[4 + k].astype(F32)
        first[48 + k] = jnp.where(upper, diagonal, 0.0).astype(BF16)
        first[56 + k] = jnp.where(lower, diagonal, 0.0).astype(BF16)
        pivots[k] = reciprocal(diagonal)
        return carry

    lax.fori_loop(0, 8, prepare, 0, unroll=2)

    def begin(k, carry):
        t = plan[TILES + k] & 255
        work[t] = first[(t >> 3) * ROWS + (t & 7) + 4].astype(F32)
        return carry

    lax.fori_loop(0, plan[2], begin, 0)

    def multiply(k, carry):
        entries = entries_of(plan, LIST1, k)
        products = [jnp.dot(first[e & 255], first[(e >> 8) & 255], preferred_element_type=F32) for e in entries]
        for e, product in zip(entries, products):
            work[e >> 16] -= product
        return carry

    lax.fori_loop(0, (plan[0] + STEP - 1) // STEP, multiply, 0)

    def scaled(tile, kind, row):
        factor = jnp.where((kind == 1) | ((kind == 2) & lower), row, 1.0)
        return tile * factor

    def split(t, tile):
        top = tile.astype(BF16)
        high[t] = top
        low[t] = (tile - top.astype(F32)).astype(BF16)

    def finish(k, carry):
        entry = plan[TILES + k]
        t, kind, diagonal = entry & 255, (entry >> 8) & 255, entry >> 16
        tile = scaled(work[t], kind, pivots[diagonal])
        split(t, tile)

        @pl.when(t < 8)
        def _():
            split(32 + t, jnp.where(upper, tile, 0.0))
            split(40 + t, jnp.where(lower, tile, 0.0))
            pivots_next[t] = reciprocal(tile)

        return carry

    lax.fori_loop(0, plan[2], finish, 0)
    out[...] = coarse[...]

    def again(k, carry):
        entries = entries_of(plan, LIST2, k)
        products = []
        for e in entries:
            x, y = e & 255, (e >> 8) & 255
            product = jnp.dot(high[x], high[y], preferred_element_type=F32)
            product += jnp.dot(high[x], low[y], preferred_element_type=F32)
            products.append(product + jnp.dot(low[x], high[y], preferred_element_type=F32))
        for e, product in zip(entries, products):
            out[e >> 16] -= product
        return carry

    lax.fori_loop(0, (plan[1] + STEP - 1) // STEP, again, 0)
    for r in range(4):
        entry = plan[KINDS + r]
        out[r] = scaled(out[r], entry & 255, pivots_next[entry >> 8])


def along(block, axis, distance, ring=False, sources=None):
    count = lax.axis_size(axis)
    pairs = [(i, (i + distance) % count) for i in range(count) if ring or 0 <= i + distance < count]
    return lax.ppermute(block, axis, [pair for pair in pairs if sources is None or pair[0] in sources])


def on_device(fine_tiles, fine_cols, agg_of, prolong, coarse_cols):
    rows, width = prolong.shape[0], prolong.shape[-1]
    agg, col = lax.axis_index("agg"), lax.axis_index("col")
    ids = jnp.stack([agg, col]).astype(jnp.int32)
    packed = packed_shape(width)
    four, four_packed = (4, width, width), (4, *packed)

    def array(shape, dtype):
        return jax.ShapeDtypeStruct(shape, dtype)

    def call(kernel, ins, outs, out_specs, scratch, name, mebibytes):
        return pl.pallas_call(
            kernel,
            out_shape=outs,
            in_specs=ins,
            out_specs=out_specs,
            scratch_shapes=scratch,
            name=name,
            compiler_params=pltpu.CompilerParams(vmem_limit_bytes=mebibytes << 20),
        )

    cols = fine_cols.reshape(-1)
    tiles = fine_tiles.reshape(rows, width, width)
    halo_shape = (rows * packed[0] + 16, 128)
    halo = call(pack_kernel, [SMEM] * 2 + [VMEM], array(halo_shape, BF16), VMEM, [], "pack", 60)(
        agg_of, coarse_cols, prolong
    )
    left, right = along(halo, "agg", 1), along(halo, "agg", -1)
    total, turned = call(
        close_kernel,
        [SMEM] * 4 + [VMEM] * 2,
        (array((SPARE + 1, width, width), F32), array((rows, width, width), BF16)),
        (VMEM, VMEM),
        [pltpu.SMEM((20,), jnp.int32)],
        "close",
        14,
    )(ids, cols, agg_of, coarse_cols, tiles, prolong)
    mine, ahead, behind, near = call(
        distant_kernel,
        [SMEM] * 4 + [VMEM] * 5,
        (array(four, F32), array(four_packed, BF16), array(four_packed, BF16), array((16,), jnp.int32)),
        (VMEM, VMEM, VMEM, SMEM),
        [
            pltpu.VMEM((SPARE + 1, width, width), F32),
            pltpu.VMEM((STEP, width, width), BF16),
            pltpu.VMEM((32, 128), jnp.int32),
            pltpu.SMEM((32, 128), jnp.int32),
            pltpu.SMEM((20,), jnp.int32),
            pltpu.SemaphoreType.DMA,
        ],
        "distant",
        22,
    )(ids, cols, agg_of, coarse_cols, tiles, turned, left, right, total)

    came_ahead = lax.ppermute(ahead, "col", [(1, 2), (2, 3), (3, 1)])
    came_behind = lax.ppermute(behind, "col", [(1, 3), (2, 1), (3, 2)])
    far = along(near, "agg", 1)
    plan = call(
        plan_kernel,
        [SMEM] * 4,
        array((PLAN,), jnp.int32),
        SMEM,
        [pltpu.SMEM((48,), jnp.int32), pltpu.SMEM((32,), jnp.int32)],
        "plan",
        4,
    )(ids, coarse_cols, near, far)
    coarse, sent, kept = call(
        combine_kernel,
        [SMEM] + [VMEM] * 3,
        (array(four, F32), array(four_packed, BF16), array(four, F32)),
        (VMEM, VMEM, VMEM),
        [pltpu.VMEM((width, width), F32)],
        "combine",
        8,
    )(plan, mine, came_ahead, came_behind)

    here = [sent] + [along(sent, "col", d, True) for d in (1, -1, 2)]
    before = [along(x, "agg", 1) for x in here]
    others = (1, 2, 3)
    second = along(sent, "agg", 2)
    further = [second] + [along(second, "col", d, True, others) for d in (1, -1)] + [along(before[3], "agg", 1)]
    factor = call(
        sweep_kernel,
        [SMEM] * 2 + [VMEM] * 13,
        array(four, F32),
        VMEM,
        [
            pltpu.VMEM((65, width, width), BF16),
            pltpu.VMEM((33, width, width), F32),
            pltpu.VMEM((49, width, width), BF16),
            pltpu.VMEM((49, width, width), BF16),
            pltpu.VMEM((8, 1, width), F32),
            pltpu.VMEM((8, 1, width), F32),
        ],
        "sweep",
        34,
    )(ids, plan, kept, *further, *before, *here)
    return (coarse[:, None], factor[:, None])


def solution(mesh):
    in_specs = (
        P("agg", "col", None, None),
        P("agg", "col"),
        P("agg"),
        P("agg", None, None),
        P("agg", None),
    )
    out_specs = (P("agg", "col", None, None), P("agg", "col", None, None))
    return jax.shard_map(
        on_device, mesh=mesh, in_specs=in_specs, out_specs=out_specs, check_vma=False
    )
```

```python
import functools

import jax
import jax.numpy as jnp
from jax import lax
from jax.experimental import pallas as pl
from jax.experimental.pallas import tpu as pltpu
from jax.sharding import PartitionSpec as P

F32 = jnp.float32
BF16 = jnp.bfloat16
VMEM = pl.BlockSpec(memory_space=pltpu.VMEM)
SMEM = pl.BlockSpec(memory_space=pltpu.SMEM)
ANY = pl.BlockSpec(memory_space=pl.ANY)

ROWS = 12
LIST1 = 16
LIST2 = 160
TILES = 192
KINDS = 240
PLAN = 256
STEP = 4
ZERO1 = 64
ZERO2 = 48
SPARE = 16


def iota(shape, dim):
    return lax.broadcasted_iota(jnp.int32, shape, dim)


def packed_shape(width):
    return (width * width // 128, 128)


def store_packed(ref, tile):
    width, half = tile.shape[0], tile.shape[0] // 2
    ref[:width] = tile[:, :128]
    ref[width:] = jnp.concatenate([tile[:half, 128:], tile[half:, 128:]], axis=1)


def store_unpacked(ref, packed, width):
    half, rest = width // 2, width - 128
    ref[:, :128] = packed[:width]
    ref[:half, 128:] = packed[width:, :rest]
    ref[half:, 128:] = packed[width:, rest:]


def pack_kernel(labels, pattern, tiles, packed):
    count, size = tiles.shape[0], tiles.shape[1] * tiles.shape[2] // 128
    line, lane = iota((16, 128), 0), iota((16, 128), 1)
    about = jnp.zeros((16, 128), F32)
    for i in range(count):
        about = jnp.where((line == 0) & (lane == i), (labels[i] & 3).astype(F32), about)
    for r in range(4):
        for q in range(1, 4):
            offset = pattern[r, q] - pattern[r, 0]
            about = jnp.where((line == 1) & (lane == 4 * r + q), offset.astype(F32), about)
    packed[count * size :] = about.astype(BF16)
    for i in range(count):
        store_packed(packed.at[pl.ds(i * size, size)], tiles[i])


def entries_of(plan, start, k):
    return [plan[start + STEP * k + u] for u in range(STEP)]


def add_lifted(entries, tiles, turned, remote, total):
    carried = [
        jnp.dot(tiles[e & 255], remote(u, (e >> 8) & 255), preferred_element_type=F32).astype(BF16)
        for u, e in enumerate(entries)
    ]
    lifted = [
        jnp.dot(turned[e & 255], c, preferred_element_type=F32) for e, c in zip(entries, carried)
    ]
    for e, tile in zip(entries, lifted):
        total[e >> 16] += tile


def slot_of(pattern, row, target):
    slot = jnp.int32(0)
    for q in range(1, 4):
        slot = jnp.where(pattern[row, q] == target, q, slot)
    return slot


def close_kernel(ids, cols, labels, pattern, tiles, own, total, turned, work):
    agg = ids[0]

    def note(i, count):
        place = cols[i] - agg * 16
        row = labels[i] & 3
        slot = slot_of(pattern, row, labels[place & 15])
        work[count] = i | ((place & 15) << 8) | ((slot * 4 + row) << 16)
        return count + (place >> 4 == 0).astype(jnp.int32)

    count = lax.fori_loop(0, 16, note, jnp.int32(0))
    for u in range(STEP - 1):
        work[count + u] = SPARE << 16
    total[...] = jnp.zeros_like(total)

    def turn(i, carry):
        turned[i] = own[i].T
        return carry

    lax.fori_loop(0, 16, turn, 0)

    def step(k, carry):
        add_lifted(entries_of(work, 0, k), tiles, turned, lambda u, place: own[place], total)
        return carry

    lax.fori_loop(0, (count + STEP - 1) // STEP, step, 0)


def distant_kernel(ids, cols, labels, pattern, tiles, turned, left, right, begun, *refs):
    mine, ahead, behind, near, total, remote, seen, about, work, sem = refs
    agg, col = ids[0], ids[1]
    width = tiles.shape[-1]
    size = width * width // 128
    end = 16 * size
    seen[:16] = left[end:].astype(F32).astype(jnp.int32)
    seen[16:] = right[end:].astype(F32).astype(jnp.int32)
    copy = pltpu.make_async_copy(seen, about, sem)
    copy.start()
    total[...] = begun[...]
    copy.wait()

    def note(i, count):
        place = cols[i] - (agg - 1) * 16
        side, within = place >> 4, place & 15
        target = jnp.where(side == 0, about[0, within] + 4 * agg - 4, about[16, within] + 4 * agg + 4)
        row = labels[i] & 3
        slot = slot_of(pattern, row, target)
        work[count] = i | ((within + jnp.where(side == 0, 0, 16)) << 8) | ((slot * 4 + row) << 16)
        return count + (side != 1).astype(jnp.int32)

    count = lax.fori_loop(0, 16, note, jnp.int32(0))
    for u in range(STEP - 1):
        work[count + u] = SPARE << 16
    for k in range(16):
        near[k] = 4 * agg - 4 + k // 4 + about[1, k]

    def step(k, carry):
        entries = entries_of(work, 0, k)
        for u, e in enumerate(entries):
            place = (e >> 8) & 255
            start = pl.multiple_of((place & 15) * size, 16)

            @pl.when(place < 16)
            def _():
                store_unpacked(remote.at[u], left[pl.ds(start, size)], width)

            @pl.when(place >= 16)
            def _():
                store_unpacked(remote.at[u], right[pl.ds(start, size)], width)

        add_lifted(entries, tiles, turned, lambda u, place: remote[u], total)
        return carry

    lax.fori_loop(0, (count + STEP - 1) // STEP, step, 0)
    first = jnp.where(col == 3, 1, col + 1)
    second = jnp.where(col <= 1, 3, col - 1)
    for r in range(4):
        mine[r] = total[col * 4 + r]
        store_packed(ahead.at[r], total[first * 4 + r].astype(BF16))
        store_packed(behind.at[r], total[second * 4 + r].astype(BF16))


def combine_kernel(plan, mine, ahead, behind, coarse, sent, kept, wide):
    width = mine.shape[-1]
    for r in range(4):
        store_unpacked(wide, ahead[r].astype(F32) + behind[r].astype(F32), width)
        tile = mine[r] + wide[...]
        coarse[r] = tile
        kept[r] = tile
        store_packed(sent.at[r], tile.astype(BF16))


def plan_kernel(ids, pattern, near, far, plan, pat, need):
    agg, col = ids[0], ids[1]
    base = (agg - 2) * 4
    for k in range(16):
        pat[k] = far[k]
        pat[16 + k] = near[k]
        pat[32 + k] = pattern[k // 4, k % 4]
    for k in range(32):
        need[k] = 0

    def through(row, index, target, m):
        inner = pat[4 * row + m]
        at = jnp.clip(inner - base, 0, ROWS - 1)
        n = jnp.int32(0)
        for q in range(1, 4):
            n = jnp.where(pat[4 * at + q] == target, q, n)
        valid = (inner < jnp.minimum(index, target)) & (n > 0)
        return at, n, valid

    count = jnp.int32(0)
    for r in range(4):
        row = 8 + r
        index = base + row
        target = pat[4 * row + col]
        lower = target < index
        diagonal = jnp.where(lower, jnp.clip(target - base, 4, ROWS - 1), row) - 4
        need[col * 8 + row - 4] = 1
        need[diagonal] = 1
        for m in range(1, 4):
            at, n, valid = through(row, index, target, m)
            x, y = m * 8 + row - 4, n * 8 + jnp.maximum(at - 4, 0)
            plan[LIST2 + count] = x | (y << 8) | (r << 16)
            count = count + valid.astype(jnp.int32)

            @pl.when(valid)
            def _():
                need[x] = 1
                need[y] = 1

        own = col * 8 + row - 4
        x = jnp.where(lower, own, 40 + row - 4)
        y = jnp.where(target > index, own, 32 + diagonal)
        plan[LIST2 + count] = x | (y << 8) | (r << 16)
        count = count + 1
        kind = jnp.where(lower, 1, jnp.where(target == index, 2, 0))
        plan[KINDS + r] = kind | (diagonal << 8)
    plan[1] = count
    for u in range(STEP - 1):
        plan[LIST2 + count + u] = ZERO2 | (ZERO2 << 8)

    def tile(t, carry):
        @pl.when(need[t] == 1)
        def _():
            products, tiles = plan[0], plan[2]
            row = (t & 7) + 4
            slot = t >> 3
            index = base + row
            target = pat[4 * row + slot]
            lower = target < index
            diagonal = jnp.where(lower, jnp.clip(target - base, 4, ROWS - 1), row) - 4
            for m in range(1, 4):
                at, n, valid = through(row, index, target, m)
                plan[LIST1 + products] = (m * ROWS + row) | ((n * ROWS + at) << 8) | (t << 16)
                products = products + valid.astype(jnp.int32)
            own = slot * ROWS + row
            x = jnp.where(lower, own, 56 + row - 4)
            y = jnp.where(target > index, own, 48 + diagonal)
            plan[LIST1 + products] = x | (y << 8) | (t << 16)
            plan[0] = products + 1
            kind = jnp.where(lower, 1, jnp.where(target == index, 2, 0))
            plan[TILES + tiles] = t | (kind << 8) | (diagonal << 16)
            plan[2] = tiles + 1

        return carry

    plan[0] = 0
    plan[2] = 0
    lax.fori_loop(0, 32, tile, 0)
    for u in range(2 * STEP - 1):
        plan[LIST1 + plan[0] + u] = ZERO1 | (ZERO1 << 8) | (32 << 16)


def sweep_kernel(ids, plan, coarse, *refs):
    pieces, (out, first, work, high, low, pivots, pivots_next) = refs[:12], refs[12:]
    col = ids[1]
    width = coarse.shape[-1]
    first[ZERO1] = jnp.zeros((width, width), BF16)
    high[ZERO2] = jnp.zeros((width, width), BF16)
    low[ZERO2] = jnp.zeros((width, width), BF16)
    lines, columns = iota((width, width), 0), iota((width, width), 1)
    upper, lower, equal = columns > lines, lines > columns, lines == columns

    def reciprocal(tile):
        return 1.0 / jnp.maximum(jnp.sum(jnp.where(equal, tile, 0.0), axis=0, keepdims=True), 1.0)

    for k, piece in enumerate(pieces):
        start = ((col + (0, 3, 1, 2)[k % 4]) & 3) * ROWS + k // 4 * 4
        for r in range(4):
            store_unpacked(first.at[start + r], piece[r], width)

    def prepare(k, carry):
        diagonal = first[4 + k].astype(F32)
        first[48 + k] = jnp.where(upper, diagonal, 0.0).astype(BF16)
        first[56 + k] = jnp.where(lower, diagonal, 0.0).astype(BF16)
        pivots[k] = reciprocal(diagonal)
        return carry

    lax.fori_loop(0, 8, prepare, 0, unroll=2)

    def begin(k, carry):
        t = plan[TILES + k] & 255
        work[t] = first[(t >> 3) * ROWS + (t & 7) + 4].astype(F32)
        return carry

    lax.fori_loop(0, plan[2], begin, 0)

    def multiply(k, carry):
        entries = entries_of(plan, LIST1, 2 * k) + entries_of(plan, LIST1, 2 * k + 1)
        products = [jnp.dot(first[e & 255], first[(e >> 8) & 255], preferred_element_type=F32) for e in entries]
        for e, product in zip(entries, products):
            work[e >> 16] -= product
        return carry

    lax.fori_loop(0, (plan[0] + 2 * STEP - 1) // (2 * STEP), multiply, 0)

    def scaled(tile, kind, row):
        factor = jnp.where((kind == 1) | ((kind == 2) & lower), row, 1.0)
        return tile * factor

    def split(t, tile):
        top = tile.astype(BF16)
        high[t] = top
        low[t] = (tile - top.astype(F32)).astype(BF16)

    def finish(k, carry):
        entry = plan[TILES + k]
        t, kind, diagonal = entry & 255, (entry >> 8) & 255, entry >> 16
        tile = scaled(work[t], kind, pivots[diagonal])
        split(t, tile)

        @pl.when(t < 8)
        def _():
            split(32 + t, jnp.where(upper, tile, 0.0))
            split(40 + t, jnp.where(lower, tile, 0.0))
            pivots_next[t] = reciprocal(tile)

        return carry

    lax.fori_loop(0, plan[2], finish, 0)
    out[...] = coarse[...]

    def again(k, carry):
        entries = entries_of(plan, LIST2, k)
        products = []
        for e in entries:
            x, y = e & 255, (e >> 8) & 255
            product = jnp.dot(high[x], high[y], preferred_element_type=F32)
            product += jnp.dot(high[x], low[y], preferred_element_type=F32)
            products.append(product + jnp.dot(low[x], high[y], preferred_element_type=F32))
        for e, product in zip(entries, products):
            out[e >> 16] -= product
        return carry

    lax.fori_loop(0, (plan[1] + STEP - 1) // STEP, again, 0)
    for r in range(4):
        entry = plan[KINDS + r]
        out[r] = scaled(out[r], entry & 255, pivots_next[entry >> 8])


def along(block, axis, distance, ring=False, sources=None):
    count = lax.axis_size(axis)
    pairs = [(i, (i + distance) % count) for i in range(count) if ring or 0 <= i + distance < count]
    return lax.ppermute(block, axis, [pair for pair in pairs if sources is None or pair[0] in sources])


def on_device(fine_tiles, fine_cols, agg_of, prolong, coarse_cols):
    rows, width = prolong.shape[0], prolong.shape[-1]
    agg, col = lax.axis_index("agg"), lax.axis_index("col")
    ids = jnp.stack([agg, col]).astype(jnp.int32)
    packed = packed_shape(width)
    four, four_packed = (4, width, width), (4, *packed)

    def array(shape, dtype):
        return jax.ShapeDtypeStruct(shape, dtype)

    def call(kernel, ins, outs, out_specs, scratch, name, mebibytes):
        return pl.pallas_call(
            kernel,
            out_shape=outs,
            in_specs=ins,
            out_specs=out_specs,
            scratch_shapes=scratch,
            name=name,
            compiler_params=pltpu.CompilerParams(vmem_limit_bytes=mebibytes << 20),
        )

    cols = fine_cols.reshape(-1)
    tiles = fine_tiles.reshape(rows, width, width)
    halo_shape = (rows * packed[0] + 16, 128)
    halo = call(pack_kernel, [SMEM] * 2 + [VMEM], array(halo_shape, BF16), VMEM, [], "pack", 60)(
        agg_of, coarse_cols, prolong
    )
    left, right = along(halo, "agg", 1), along(halo, "agg", -1)
    total, turned = call(
        close_kernel,
        [SMEM] * 4 + [VMEM] * 2,
        (array((SPARE + 1, width, width), F32), array((rows, width, width), BF16)),
        (VMEM, VMEM),
        [pltpu.SMEM((20,), jnp.int32)],
        "close",
        14,
    )(ids, cols, agg_of, coarse_cols, tiles, prolong)
    mine, ahead, behind, near = call(
        distant_kernel,
        [SMEM] * 4 + [VMEM] * 5,
        (array(four, F32), array(four_packed, BF16), array(four_packed, BF16), array((16,), jnp.int32)),
        (VMEM, VMEM, VMEM, SMEM),
        [
            pltpu.VMEM((SPARE + 1, width, width), F32),
            pltpu.VMEM((STEP, width, width), BF16),
            pltpu.VMEM((32, 128), jnp.int32),
            pltpu.SMEM((32, 128), jnp.int32),
            pltpu.SMEM((20,), jnp.int32),
            pltpu.SemaphoreType.DMA,
        ],
        "distant",
        22,
    )(ids, cols, agg_of, coarse_cols, tiles, turned, left, right, total)

    came_ahead = lax.ppermute(ahead, "col", [(1, 2), (2, 3), (3, 1)])
    came_behind = lax.ppermute(behind, "col", [(1, 3), (2, 1), (3, 2)])
    far = along(near, "agg", 1)
    plan = call(
        plan_kernel,
        [SMEM] * 4,
        array((PLAN,), jnp.int32),
        SMEM,
        [pltpu.SMEM((48,), jnp.int32), pltpu.SMEM((32,), jnp.int32)],
        "plan",
        4,
    )(ids, coarse_cols, near, far)
    coarse, sent, kept = call(
        combine_kernel,
        [SMEM] + [VMEM] * 3,
        (array(four, F32), array(four_packed, BF16), array(four, F32)),
        (VMEM, VMEM, VMEM),
        [pltpu.VMEM((width, width), F32)],
        "combine",
        8,
    )(plan, mine, came_ahead, came_behind)

    here = [sent] + [along(sent, "col", d, True) for d in (1, -1, 2)]
    before = [along(x, "agg", 1) for x in here]
    others = (1, 2, 3)
    second = along(sent, "agg", 2)
    further = [second] + [along(second, "col", d, True, others) for d in (1, -1)] + [along(before[3], "agg", 1)]
    factor = call(
        sweep_kernel,
        [SMEM] * 2 + [VMEM] * 13,
        array(four, F32),
        VMEM,
        [
            pltpu.VMEM((65, width, width), BF16),
            pltpu.VMEM((33, width, width), F32),
            pltpu.VMEM((49, width, width), BF16),
            pltpu.VMEM((49, width, width), BF16),
            pltpu.VMEM((8, 1, width), F32),
            pltpu.VMEM((8, 1, width), F32),
        ],
        "sweep",
        34,
    )(ids, plan, kept, *further, *before, *here)
    return (coarse[:, None], factor[:, None])


def solution(mesh):
    in_specs = (
        P("agg", "col", None, None),
        P("agg", "col"),
        P("agg"),
        P("agg", None, None),
        P("agg", None),
    )
    out_specs = (P("agg", "col", None, None), P("agg", "col", None, None))
    return jax.shard_map(
        on_device, mesh=mesh, in_specs=in_specs, out_specs=out_specs, check_vma=False
    )
```
